512 devices in a mesh: row: 32 (over y, x), col: 16 (over z, core).
Axes of the slice: x: 4, y: 8, z: 8, core: 2. Of those that a mesh axis runs over, the one named last changes fastest.
Arguments:
- tensor: float32 [512, 256, 2048], P(None, 'row', 'col'), may hold values from -60 to 60, as said below
- initial_basis: float32 [512, 128], replicated, may hold values from -6 to 6
Outputs:
- factor: float32 [512, 128], replicated
- core_tensor: float32 [128, 256, 2048], P(None, 'row', 'col')
The draws below stay inside these ranges and needn't reach their ends.
Inputs may be any that keep to these rules, and one draw needn't show every extreme that they name: Entries of the data tensor.
All inputs are finite; a program needn't handle non-finite values.
Results may differ from the reference program's by a relative error of at most 0.00015.
Values sent between devices are 32-bit elements; how exact they have to be, the bound alone decides.
A program may use at most 64 MiB of HBM per device.

```python
import math
import jax
import jax.numpy as jnp
from jax import lax

I1 = 512
RANK = 128
ITERS = 3
I2 = 256
I3 = 2048


def draw_tensor(key, part):
    subkeys = jax.random.split(key, 4)
    full_shape = (I1, I2, I3)
    random_part = jnp.clip(jax.random.normal(subkeys[0], full_shape, jnp.float32), -4.0, 4.0)
    low_scale = 0.5
    high_scale = 2.0
    coupled = random_part + 0.5 * jnp.roll(random_part, 1, axis=0)
    row_scale = jnp.exp(jax.random.uniform(subkeys[1], (I1, I2, 1), jnp.float32, math.log(low_scale), math.log(high_scale)))
    cell_scale = jnp.exp(jax.random.uniform(subkeys[2], (1, I2, I3), jnp.float32, math.log(0.3), math.log(3.0)))
    along_two = 1.0 + 2.0 * jnp.arange(I2, dtype=jnp.float32) / (I2 - 1)
    along_three = 1.0 + 2.0 * jnp.arange(I3, dtype=jnp.float32) / (I3 - 1)
    growth = jnp.sqrt(along_two[None, :, None] * along_three[None, None, :])
    offset = jax.random.uniform(subkeys[3], (I1, 1, 1), jnp.float32, -1.0, 1.0)
    return 0.5 * row_scale * cell_scale * growth * coupled + offset


def noise(own_key, extent, width, bound, kind=jnp.bfloat16):
    return jnp.clip(width * jax.random.normal(own_key, extent, jnp.float32), -bound, bound).astype(kind)


def setup_inputs(seed: int = 0) -> dict:
    key_of = jax.random.split(jax.random.key(seed), 3)
    return {
        "tensor": draw_tensor(jax.random.fold_in(key_of[2], 71), 0),
        "initial_basis": noise(key_of[1], (I1, RANK), 1.0, 6.0, jnp.float32),
    }


def gram_of(matrix):
    return lax.dot_general(matrix.astype(jnp.float32), matrix.astype(jnp.float32), (((1,), (1,)), ((), ())), precision=lax.Precision.HIGHEST, preferred_element_type=jnp.float32)

def contract_rows(left_matrix, right_matrix):
    return lax.dot_general(left_matrix.astype(jnp.float32), right_matrix.astype(jnp.float32), (((0,), (0,)), ((), ())), precision=lax.Precision.HIGHEST, preferred_element_type=jnp.float32)

def reference(tensor, initial_basis):
    fibres = tensor.reshape(I1, I2 * I3)
    cell_count = float(I2 * I3)
    first_moment = lax.optimization_barrier(jnp.sum(fibres, axis=1))
    second_moment = lax.optimization_barrier(jnp.sum(fibres * fibres, axis=1))
    average = first_moment / cell_count
    inverse_std = 1.0 / jnp.sqrt(second_moment / cell_count - average * average + 1e-05)
    normed = (fibres - average[:, None]) * inverse_std[:, None]
    gram_matrix = gram_of(normed)
    triangle = jnp.linalg.cholesky(gram_matrix)
    basis_cols = initial_basis
    for iteration in range(ITERS):
        projected = contract_rows(triangle, basis_cols)
        power_image = jnp.dot(triangle.astype(jnp.float32), projected.astype(jnp.float32), precision=lax.Precision.HIGHEST, preferred_element_type=jnp.float32)
        small_gram = contract_rows(power_image, power_image)
        small_factor = jnp.linalg.cholesky(small_gram)
        basis_cols = lax.linalg.triangular_solve(small_factor, power_image, left_side=False, lower=True, transpose_a=True)
    core_tensor = contract_rows(basis_cols, normed).reshape(RANK, I2, I3)
    return (basis_cols, core_tensor)
```

```python
import functools

import jax
import jax.numpy as jnp
from jax import lax
from jax.experimental import pallas as pl
from jax.experimental.pallas import tpu as pltpu
from jax.sharding import PartitionSpec as P

ITERS = 3
CHIPS_X = 4
BLOCK = 128
MESH = pl.DeviceIdType.MESH
SQUARES = ((1, 0), (2, 0), (3, 0), (0, 1), (2, 1), (3, 1), (3, 2), (2, 3))
PAIRED = (3, 7)


def ring_distance(step, extent):
    return min(step, extent - step)


def far_first(extent):
    return sorted(range(1, extent), key=lambda step: -ring_distance(step, extent))


def near_first(extent):
    return sorted(range(1, extent), key=lambda step: ring_distance(step, extent))


def dot_nt(left, right, precision=None):
    return lax.dot_general(
        left, right, (((1,), (1,)), ((), ())), precision=precision, preferred_element_type=jnp.float32
    )


def gram_kernel(
    sizes, cells,
    x_hbm, gram_ref, stats_ref,
    field, high, low, local, from_core, to_x, from_x, to_z, from_z, from_y, packed,
    load_sem, core_send, core_recv, x_send, x_recv, z_send, z_recv, y_send, y_recv,
    gz_send, gz_recv, gx_send, gx_recv, gc_send, gc_recv,
):
    nx, ny, nz = sizes
    tiles_x = 64 // nx
    tiles_z = tiles_x // nz
    row, col = lax.axis_index("row"), lax.axis_index("col")
    x, y = lax.rem(row, nx), lax.div(row, nx)
    core, z = lax.rem(col, 2), lax.div(col, 2)

    def device(dx=0, dy=0, dz=0, other=False):
        to_row = lax.rem(y + dy, ny) * nx + lax.rem(x + dx, nx)
        to_col = lax.rem(z + dz, nz) * 2 + (1 - core if other else core)
        return (to_row, to_col)

    peers = [device(other=True)]
    peers += [device(dx=d) for d in range(1, nx)]
    peers += [device(dz=d) for d in range(1, nz)]
    peers += [device(dy=d) for d in range(1, ny)]
    barrier = pltpu.get_barrier_semaphore()
    for peer in peers:
        pl.semaphore_signal(barrier, inc=1, device_id=peer, device_id_type=MESH)

    def send(src, dst, send_sem, recv_sem, peer):
        copy = pltpu.make_async_remote_copy(
            src_ref=src, dst_ref=dst, send_sem=send_sem, recv_sem=recv_sem,
            device_id=peer, device_id_type=MESH,
        )
        copy.start()
        return copy

    load = pltpu.make_async_copy(x_hbm, field, load_sem)
    load.start()
    load.wait()

    rows = field.shape[0]
    slabs = field.shape[1]
    width = float(slabs * BLOCK)
    blocks = rows // BLOCK
    below = lax.broadcasted_iota(jnp.int32, (BLOCK, BLOCK), 0)
    across = lax.broadcasted_iota(jnp.int32, (BLOCK, BLOCK), 1)
    on_diagonal = below == across

    mean_down, mean_over, sums = [], [], []
    for b in range(blocks):
        here = pl.ds(b * BLOCK, BLOCK)
        total = field[here, 0, :]
        for s in range(1, slabs):
            total = total + field[here, s, :]
        total = jnp.broadcast_to(jnp.sum(total, axis=1, keepdims=True), (BLOCK, BLOCK))
        mean = total * (1.0 / width)
        for s in range(slabs):
            centred = field[here, s, :] - mean
            top = centred.astype(jnp.bfloat16)
            high[here, pl.ds(s * BLOCK, BLOCK)] = top
            low[here, pl.ds(s * BLOCK, BLOCK)] = (centred - top.astype(jnp.float32)).astype(jnp.bfloat16)
        turned = total.T
        mean_down.append(mean)
        mean_over.append(turned * (1.0 / width))
        sums.append(turned[0:1, :])

    pair = 2 * BLOCK
    square = {}
    for bi in range(blocks // 2):
        for bj in range(bi + 1):
            left, right = pl.ds(bi * pair, pair), pl.ds(bj * pair, pair)
            value = dot_nt(high[left, :], high[right, :])
            value = value + dot_nt(high[left, :], low[right, :])
            value = value + dot_nt(low[left, :], high[right, :])
            for i in range(2):
                for j in range(2):
                    r, q = 2 * bi + i, 2 * bj + j
                    if r >= q:
                        square[r, q] = value[i * BLOCK:(i + 1) * BLOCK, j * BLOCK:(j + 1) * BLOCK] + (
                            width * mean_down[r] * mean_over[q]
                        )

    def diagonal_of(block):
        return jnp.sum(jnp.where(on_diagonal, block, 0.0), axis=0, keepdims=True)

    extra = jnp.concatenate(
        sums + [diagonal_of(square[0, 0]), diagonal_of(square[2, 2]), jnp.zeros((2, BLOCK), jnp.float32)], axis=0
    )
    for index, (r, q) in enumerate(SQUARES):
        half, slot = index // 4, (index % 4) * 16
        if index in PAIRED:
            first, second = min(r, q), max(r, q)
            block = jnp.where(below > across, square[first, first], square[second, second])
        else:
            block = square[r, q]
        local[half, slot // tiles_x, pl.ds(slot % tiles_x, 16)] = block.reshape(16, 8, BLOCK)
    for half in range(2):
        for piece in range(nx):
            local[half, piece, tiles_x] = extra

    pl.semaphore_wait(barrier, len(peers))

    order_x = far_first(nx) + [0]
    partner = device(other=True)
    sent = []
    core_copies = {}
    for d in order_x:
        core_copies[d] = send(
            local.at[1 - core, lax.rem(x + d, nx)], from_core.at[d], core_send.at[d], core_recv.at[d], partner
        )
    sent += list(core_copies.values())
    x_copies = {}
    for d in order_x:
        core_copies[d].wait_recv()
        value = local[core, lax.rem(x + d, nx)] + from_core[d]
        if d == 0:
            from_x[0] = value
        else:
            to_x[d - 1] = value
            x_copies[d] = send(to_x.at[d - 1], from_x.at[d], x_send.at[d - 1], x_recv.at[d - 1], device(dx=d))
    sent += list(x_copies.values())
    for d in near_first(nx):
        x_copies[d].wait_recv()

    def x_sum(window):
        value = from_x[lax.rem(x + nx, nx), window]
        for j in range(1, nx):
            value = value + from_x[lax.rem(x + nx - j, nx), window]
        return value

    moments = x_sum(pl.ds(tiles_x, 1))
    z_copies = {}
    for d in far_first(nz) + [0]:
        value = x_sum(pl.ds(lax.rem(z + d, nz) * tiles_z, tiles_z))
        if d == 0:
            from_z[0, pl.ds(0, tiles_z)] = value
            from_z[0, pl.ds(tiles_z, 1)] = moments
        else:
            to_z[d - 1, pl.ds(0, tiles_z)] = value
            to_z[d - 1, pl.ds(tiles_z, 1)] = moments
            z_copies[d] = send(to_z.at[d - 1], from_z.at[d], z_send.at[d - 1], z_recv.at[d - 1], device(dz=d))
    sent += list(z_copies.values())
    for d in near_first(nz):
        z_copies[d].wait_recv()
    value = from_z[z]
    for j in range(1, nz):
        value = value + from_z[lax.rem(z + nz - j, nz)]
    from_y[0] = value
    y_copies = {}
    for d in far_first(ny):
        y_copies[d] = send(from_y.at[0], from_y.at[d], y_send.at[d - 1], y_recv.at[d - 1], device(dy=d))
    sent += list(y_copies.values())
    for d in near_first(ny):
        y_copies[d].wait_recv()
    value = from_y[y]
    for j in range(1, ny):
        value = value + from_y[lax.rem(y + ny - j, ny)]

    def place(dx, dz):
        tile = 64 * core + tiles_x * lax.rem(x + nx - dx, nx) + tiles_z * lax.rem(z + nz - dz, nz)
        return packed.at[pl.ds(tile, tiles_z)]

    packed[pl.ds(64 * core + tiles_x * x + tiles_z * z, tiles_z)] = value[0:tiles_z]
    extra = value[tiles_z]

    gz, gx, gc = {}, {}, {}
    mine = place(0, 0)
    for d in far_first(nz):
        gz[d] = send(mine, mine, gz_send.at[d - 1], gz_recv.at[d - 1], device(dz=d))

    def pass_on(dx, dz):
        piece = place(dx, dz)
        if dx == 0:
            for d in far_first(nx):
                gx[d, dz] = send(piece, piece, gx_send.at[d - 1, dz], gx_recv.at[d - 1, dz], device(dx=d))
        gc[dx, dz] = send(piece, piece, gc_send.at[dx, dz], gc_recv.at[dx, dz], partner)

    pass_on(0, 0)
    arrivals = [(1.0 + ring_distance(d, nz), 0, d) for d in range(1, nz)]
    arrivals += [
        ((1.0 + ring_distance(d, nz) if d else 0.0) + 1.0 + ring_distance(e, nx), e, d)
        for e in range(1, nx) for d in range(nz)
    ]
    for _, e, d in sorted(arrivals):
        if e == 0:
            gz[d].wait_recv()
        else:
            gx[e, d].wait_recv()
        pass_on(e, d)
    for copy in gc.values():
        copy.wait_recv()

    means, scales, seconds = [], [], []
    def matrix(index):
        return packed[pl.ds(16 * index, 16)].reshape(BLOCK, BLOCK)

    whole = {}
    for index, (r, q) in enumerate(SQUARES):
        block = matrix(index)
        if index in PAIRED:
            first, second = min(r, q), max(r, q)
            turned = block.T
            line = extra[4 + first // 2:5 + first // 2, :]
            whole[first, first] = jnp.where(
                below > across, block, jnp.where(below < across, turned, jnp.broadcast_to(line, (BLOCK, BLOCK)))
            )
            whole[second, second] = jnp.where(below <= across, block, turned)
        else:
            whole[r, q] = block
    for b in range(blocks):
        average = extra[b:b + 1, :] / cells
        if b % 2 == 0:
            second = extra[4 + b // 2:5 + b // 2, :]
        else:
            second = diagonal_of(whole[b, b])
        scale = 1.0 / jnp.sqrt(second / cells - average * average + 1e-05)
        stats_ref[b:b + 1, :] = average
        stats_ref[4 + b:5 + b, :] = scale
        means.append(jnp.broadcast_to(average, (BLOCK, BLOCK)))
        scales.append(jnp.broadcast_to(scale, (BLOCK, BLOCK)))
    means_down = [value.T for value in means]
    scales_down = [value.T for value in scales]
    for (r, q), block in whole.items():
        value = (block - cells * (means_down[r] * means[q])) * scales_down[r] * scales[q]
        gram_ref[pl.ds(r * BLOCK, BLOCK), pl.ds(q * BLOCK, BLOCK)] = value
        if r != q:
            gram_ref[pl.ds(q * BLOCK, BLOCK), pl.ds(r * BLOCK, BLOCK)] = value.T

    for copy in sent + list(gz.values()) + list(gx.values()) + list(gc.values()):
        copy.wait_send()


def gram_call(tensor, sizes, cells):
    nx, ny, nz = sizes
    rows, slabs, lanes = tensor.shape
    tiles_x = 64 // nx
    tiles_z = tiles_x // nz
    f32, bf16 = jnp.float32, jnp.bfloat16
    vmem = pltpu.VMEM
    dma = pltpu.SemaphoreType.DMA
    return pl.pallas_call(
        functools.partial(gram_kernel, sizes, cells),
        out_shape=(
            jax.ShapeDtypeStruct((rows, rows), f32),
            jax.ShapeDtypeStruct((8, lanes), f32),
        ),
        in_specs=[pl.BlockSpec(memory_space=pl.ANY)],
        out_specs=(pl.BlockSpec(memory_space=pltpu.VMEM), pl.BlockSpec(memory_space=pltpu.VMEM)),
        scratch_shapes=[
            vmem((rows, slabs, lanes), f32),
            vmem((rows, slabs * lanes), bf16),
            vmem((rows, slabs * lanes), bf16),
            vmem((2, nx, tiles_x + 1, 8, lanes), f32),
            vmem((nx, tiles_x + 1, 8, lanes), f32),
            vmem((nx - 1, tiles_x + 1, 8, lanes), f32),
            vmem((nx, tiles_x + 1, 8, lanes), f32),
            vmem((nz - 1, tiles_z + 1, 8, lanes), f32),
            vmem((nz, tiles_z + 1, 8, lanes), f32),
            vmem((ny, tiles_z + 1, 8, lanes), f32),
            vmem((128, 8, lanes), f32),
            dma,
            dma((nx,)), dma((nx,)),
            dma((nx - 1,)), dma((nx - 1,)),
            dma((nz - 1,)), dma((nz - 1,)),
            dma((ny - 1,)), dma((ny - 1,)),
            dma((nz - 1,)), dma((nz - 1,)),
            dma((nx - 1, nz)), dma((nx - 1, nz)),
            dma((nx, nz)), dma((nx, nz)),
        ],
        compiler_params=pltpu.CompilerParams(collective_id=0, has_side_effects=True),
    )(tensor)


def contract_rows(left_matrix, right_matrix):
    return lax.dot_general(
        left_matrix,
        right_matrix,
        (((0,), (0,)), ((), ())),
        precision=lax.Precision.HIGHEST,
        preferred_element_type=jnp.float32,
    )


def local_step(sizes, tensor, initial_basis):
    rows = tensor.shape[0]
    cells = float(tensor.shape[1] * tensor.shape[2] * lax.axis_size("row") * lax.axis_size("col"))
    gram_matrix, stats = gram_call(tensor, sizes, cells)
    average, inverse_std = stats[0:4].reshape(rows), stats[4:8].reshape(rows)
    basis_cols = initial_basis
    for iteration in range(ITERS):
        power_image = jnp.dot(
            gram_matrix, basis_cols, precision=lax.Precision.HIGHEST, preferred_element_type=jnp.float32
        )
        small_gram = contract_rows(power_image, power_image)
        small_factor = jnp.linalg.cholesky(small_gram)
        basis_cols = lax.linalg.triangular_solve(
            small_factor, power_image, left_side=False, lower=True, transpose_a=True
        )
    normed = (tensor - average[:, None, None]) * inverse_std[:, None, None]
    core_tensor = lax.dot_general(
        basis_cols, normed, (((0,), (0,)), ((), ())),
        precision=lax.Precision.HIGHEST, preferred_element_type=jnp.float32,
    )
    return (basis_cols, core_tensor)


def solution(mesh):
    nx = CHIPS_X
    sizes = (nx, mesh.shape["row"] // nx, mesh.shape["col"] // 2)
    in_specs = (P(None, "row", "col"), P())
    out_specs = (P(), P(None, "row", "col"))
    return jax.shard_map(
        functools.partial(local_step, sizes), mesh=mesh, in_specs=in_specs, out_specs=out_specs, check_vma=False
    )
```

```python
import functools

import jax
import jax.numpy as jnp
from jax import lax
from jax.experimental import pallas as pl
from jax.experimental.pallas import tpu as pltpu
from jax.sharding import PartitionSpec as P

ITERS = 3
CHIPS_X = 4
BLOCK = 128
MESH = pl.DeviceIdType.MESH
SQUARES = ((1, 0), (2, 0), (3, 0), (0, 1), (2, 1), (3, 1), (3, 2), (2, 3))
PAIRED = (3, 7)


def ring_distance(step, extent):
    return min(step, extent - step)


def far_first(extent):
    return sorted(range(1, extent), key=lambda step: -ring_distance(step, extent))


def near_first(extent):
    return sorted(range(1, extent), key=lambda step: ring_distance(step, extent))


def dot_nt(left, right, precision=None):
    return lax.dot_general(
        left, right, (((1,), (1,)), ((), ())), precision=precision, preferred_element_type=jnp.float32
    )


def gram_kernel(
    sizes, cells,
    x_hbm, gram_ref, stats_ref, high, low,
    field, local, from_core, to_x, from_x, to_z, from_z, from_y, packed,
    load_sem, core_send, core_recv, x_send, x_recv, z_send, z_recv, y_send, y_recv,
    gz_send, gz_recv, gx_send, gx_recv, gc_send, gc_recv,
):
    nx, ny, nz = sizes
    tiles_x = 64 // nx
    tiles_z = tiles_x // nz
    row, col = lax.axis_index("row"), lax.axis_index("col")
    x, y = lax.rem(row, nx), lax.div(row, nx)
    core, z = lax.rem(col, 2), lax.div(col, 2)

    def device(dx=0, dy=0, dz=0, other=False):
        to_row = lax.rem(y + dy, ny) * nx + lax.rem(x + dx, nx)
        to_col = lax.rem(z + dz, nz) * 2 + (1 - core if other else core)
        return (to_row, to_col)

    peers = [device(other=True)]
    peers += [device(dx=d) for d in range(1, nx)]
    peers += [device(dz=d) for d in range(1, nz)]
    peers += [device(dy=d) for d in range(1, ny)]
    barrier = pltpu.get_barrier_semaphore()
    for peer in peers:
        pl.semaphore_signal(barrier, inc=1, device_id=peer, device_id_type=MESH)

    def send(src, dst, send_sem, recv_sem, peer):
        copy = pltpu.make_async_remote_copy(
            src_ref=src, dst_ref=dst, send_sem=send_sem, recv_sem=recv_sem,
            device_id=peer, device_id_type=MESH,
        )
        copy.start()
        return copy

    load = pltpu.make_async_copy(x_hbm, field, load_sem)
    load.start()
    load.wait()

    rows = field.shape[0]
    slabs = field.shape[1]
    width = float(slabs * BLOCK)
    blocks = rows // BLOCK
    below = lax.broadcasted_iota(jnp.int32, (BLOCK, BLOCK), 0)
    across = lax.broadcasted_iota(jnp.int32, (BLOCK, BLOCK), 1)
    on_diagonal = below == across

    mean_down, mean_over, sums = [], [], []
    for b in range(blocks):
        here = pl.ds(b * BLOCK, BLOCK)
        total = field[here, 0, :]
        for s in range(1, slabs):
            total = total + field[here, s, :]
        total = jnp.broadcast_to(jnp.sum(total, axis=1, keepdims=True), (BLOCK, BLOCK))
        mean = total * (1.0 / width)
        for s in range(slabs):
            centred = field[here, s, :] - mean
            top = centred.astype(jnp.bfloat16)
            high[here, pl.ds(s * BLOCK, BLOCK)] = top
            low[here, pl.ds(s * BLOCK, BLOCK)] = (centred - top.astype(jnp.float32)).astype(jnp.bfloat16)
        turned = total.T
        mean_down.append(mean)
        mean_over.append(turned * (1.0 / width))
        sums.append(turned[0:1, :])

    pair = 2 * BLOCK
    square = {}
    for bi in range(blocks // 2):
        for bj in range(bi + 1):
            left, right = pl.ds(bi * pair, pair), pl.ds(bj * pair, pair)
            value = dot_nt(high[left, :], high[right, :])
            value = value + dot_nt(high[left, :], low[right, :])
            value = value + dot_nt(low[left, :], high[right, :])
            for i in range(2):
                for j in range(2):
                    r, q = 2 * bi + i, 2 * bj + j
                    if r >= q:
                        square[r, q] = value[i * BLOCK:(i + 1) * BLOCK, j * BLOCK:(j + 1) * BLOCK] + (
                            width * mean_down[r] * mean_over[q]
                        )

    def diagonal_of(block):
        return jnp.sum(jnp.where(on_diagonal, block, 0.0), axis=0, keepdims=True)

    extra = jnp.concatenate(
        sums + [diagonal_of(square[0, 0]), diagonal_of(square[2, 2]), jnp.zeros((2, BLOCK), jnp.float32)], axis=0
    )
    for index, (r, q) in enumerate(SQUARES):
        half, slot = index // 4, (index % 4) * 16
        if index in PAIRED:
            first, second = min(r, q), max(r, q)
            block = jnp.where(below > across, square[first, first], square[second, second])
        else:
            block = square[r, q]
        local[half, slot // tiles_x, pl.ds(slot % tiles_x, 16)] = block.reshape(16, 8, BLOCK)
    for half in range(2):
        for piece in range(nx):
            local[half, piece, tiles_x] = extra

    pl.semaphore_wait(barrier, len(peers))

    order_x = far_first(nx) + [0]
    partner = device(other=True)
    sent = []
    core_copies = {}
    for d in order_x:
        core_copies[d] = send(
            local.at[1 - core, lax.rem(x + d, nx)], from_core.at[d], core_send.at[d], core_recv.at[d], partner
        )
    sent += list(core_copies.values())
    x_copies = {}
    for d in order_x:
        core_copies[d].wait_recv()
        value = local[core, lax.rem(x + d, nx)] + from_core[d]
        if d == 0:
            from_x[0] = value
        else:
            to_x[d - 1] = value
            x_copies[d] = send(to_x.at[d - 1], from_x.at[d], x_send.at[d - 1], x_recv.at[d - 1], device(dx=d))
    sent += list(x_copies.values())
    for d in near_first(nx):
        x_copies[d].wait_recv()

    def x_sum(window):
        value = from_x[lax.rem(x + nx, nx), window]
        for j in range(1, nx):
            value = value + from_x[lax.rem(x + nx - j, nx), window]
        return value

    moments = x_sum(pl.ds(tiles_x, 1))
    z_copies = {}
    for d in far_first(nz) + [0]:
        value = x_sum(pl.ds(lax.rem(z + d, nz) * tiles_z, tiles_z))
        if d == 0:
            from_z[0, pl.ds(0, tiles_z)] = value
            from_z[0, pl.ds(tiles_z, 1)] = moments
        else:
            to_z[d - 1, pl.ds(0, tiles_z)] = value
            to_z[d - 1, pl.ds(tiles_z, 1)] = moments
            z_copies[d] = send(to_z.at[d - 1], from_z.at[d], z_send.at[d - 1], z_recv.at[d - 1], device(dz=d))
    sent += list(z_copies.values())
    for d in near_first(nz):
        z_copies[d].wait_recv()
    value = from_z[z]
    for j in range(1, nz):
        value = value + from_z[lax.rem(z + nz - j, nz)]
    from_y[0] = value
    y_copies = {}
    for d in far_first(ny):
        y_copies[d] = send(from_y.at[0], from_y.at[d], y_send.at[d - 1], y_recv.at[d - 1], device(dy=d))
    sent += list(y_copies.values())
    for d in near_first(ny):
        y_copies[d].wait_recv()
    value = from_y[y]
    for j in range(1, ny):
        value = value + from_y[lax.rem(y + ny - j, ny)]

    def place(dx, dz):
        tile = 64 * core + tiles_x * lax.rem(x + nx - dx, nx) + tiles_z * lax.rem(z + nz - dz, nz)
        return packed.at[pl.ds(tile, tiles_z)]

    packed[pl.ds(64 * core + tiles_x * x + tiles_z * z, tiles_z)] = value[0:tiles_z]
    extra = value[tiles_z]

    gz, gx, gc = {}, {}, {}
    mine = place(0, 0)
    for d in far_first(nz):
        gz[d] = send(mine, mine, gz_send.at[d - 1], gz_recv.at[d - 1], device(dz=d))

    def pass_on(dx, dz):
        piece = place(dx, dz)
        if dx == 0:
            for d in far_first(nx):
                gx[d, dz] = send(piece, piece, gx_send.at[d - 1, dz], gx_recv.at[d - 1, dz], device(dx=d))
        gc[dx, dz] = send(piece, piece, gc_send.at[dx, dz], gc_recv.at[dx, dz], partner)

    pass_on(0, 0)
    arrivals = [(1.0 + ring_distance(d, nz), 0, d) for d in range(1, nz)]
    arrivals += [
        ((1.0 + ring_distance(d, nz) if d else 0.0) + 1.0 + ring_distance(e, nx), e, d)
        for e in range(1, nx) for d in range(nz)
    ]
    for _, e, d in sorted(arrivals):
        if e == 0:
            gz[d].wait_recv()
        else:
            gx[e, d].wait_recv()
        pass_on(e, d)
    for copy in gc.values():
        copy.wait_recv()

    means, scales, seconds = [], [], []
    def matrix(index):
        return packed[pl.ds(16 * index, 16)].reshape(BLOCK, BLOCK)

    whole = {}
    for index, (r, q) in enumerate(SQUARES):
        block = matrix(index)
        if index in PAIRED:
            first, second = min(r, q), max(r, q)
            turned = block.T
            line = extra[4 + first // 2:5 + first // 2, :]
            whole[first, first] = jnp.where(
                below > across, block, jnp.where(below < across, turned, jnp.broadcast_to(line, (BLOCK, BLOCK)))
            )
            whole[second, second] = jnp.where(below <= across, block, turned)
        else:
            whole[r, q] = block
    for b in range(blocks):
        average = extra[b:b + 1, :] / cells
        if b % 2 == 0:
            second = extra[4 + b // 2:5 + b // 2, :]
        else:
            second = diagonal_of(whole[b, b])
        scale = 1.0 / jnp.sqrt(second / cells - average * average + 1e-05)
        stats_ref[b:b + 1, :] = average
        stats_ref[4 + b:5 + b, :] = scale
        stats_ref[8 + b:9 + b, :] = sums[b] * (1.0 / width) - average
        means.append(jnp.broadcast_to(average, (BLOCK, BLOCK)))
        scales.append(jnp.broadcast_to(scale, (BLOCK, BLOCK)))
    stats_ref[16:24, :] = jnp.ones((8, BLOCK), jnp.float32)
    means_down = [value.T for value in means]
    scales_down = [value.T for value in scales]
    for (r, q), block in whole.items():
        value = (block * (1.0 / cells) - means_down[r] * means[q]) * scales_down[r] * scales[q]
        gram_ref[pl.ds(r * BLOCK, BLOCK), pl.ds(q * BLOCK, BLOCK)] = value
        if r != q:
            gram_ref[pl.ds(q * BLOCK, BLOCK), pl.ds(r * BLOCK, BLOCK)] = value.T

    for copy in sent + list(gz.values()) + list(gx.values()) + list(gc.values()):
        copy.wait_send()


def gram_call(tensor, sizes, cells):
    nx, ny, nz = sizes
    rows, slabs, lanes = tensor.shape
    tiles_x = 64 // nx
    tiles_z = tiles_x // nz
    f32, bf16 = jnp.float32, jnp.bfloat16
    vmem = pltpu.VMEM
    dma = pltpu.SemaphoreType.DMA
    return pl.pallas_call(
        functools.partial(gram_kernel, sizes, cells),
        out_shape=(
            jax.ShapeDtypeStruct((rows, rows), f32),
            jax.ShapeDtypeStruct((24, lanes), f32),
            jax.ShapeDtypeStruct((rows, slabs * lanes), bf16),
            jax.ShapeDtypeStruct((rows, slabs * lanes), bf16),
        ),
        in_specs=[pl.BlockSpec(memory_space=pl.ANY)],
        out_specs=(pl.BlockSpec(memory_space=pltpu.VMEM),) * 4,
        scratch_shapes=[
            vmem((rows, slabs, lanes), f32),
            vmem((2, nx, tiles_x + 1, 8, lanes), f32),
            vmem((nx, tiles_x + 1, 8, lanes), f32),
            vmem((nx - 1, tiles_x + 1, 8, lanes), f32),
            vmem((nx, tiles_x + 1, 8, lanes), f32),
            vmem((nz - 1, tiles_z + 1, 8, lanes), f32),
            vmem((nz, tiles_z + 1, 8, lanes), f32),
            vmem((ny, tiles_z + 1, 8, lanes), f32),
            vmem((128, 8, lanes), f32),
            dma,
            dma((nx,)), dma((nx,)),
            dma((nx - 1,)), dma((nx - 1,)),
            dma((nz - 1,)), dma((nz - 1,)),
            dma((ny - 1,)), dma((ny - 1,)),
            dma((nz - 1,)), dma((nz - 1,)),
            dma((nx - 1, nz)), dma((nx - 1, nz)),
            dma((nx, nz)), dma((nx, nz)),
        ],
        compiler_params=pltpu.CompilerParams(collective_id=0, has_side_effects=True),
    )(tensor)


def over(value, lane, one):
    return jnp.broadcast_to(value[:, lane:lane + 1], (8, BLOCK)) * one


def down(value, line):
    return jnp.broadcast_to(value[line:line + 1, :], (8, BLOCK))


def add_up(terms):
    while len(terms) > 1:
        terms = [terms[i] + terms[i + 1] for i in range(0, len(terms), 2)]
    return terms[0]


def inverse_factor(matrix, one):
    groups = BLOCK // 8
    line = lax.broadcasted_iota(jnp.int32, (8, BLOCK), 0)
    lane = lax.broadcasted_iota(jnp.int32, (8, BLOCK), 1)
    a = [matrix[8 * v:8 * v + 8, :] for v in range(groups)]
    w = [jnp.where(lane == line + 8 * v, 1.0, 0.0).astype(jnp.float32) for v in range(groups)]
    result = []
    panel = [over(a[0], m, one) for m in range(8)]
    under = [over(a[1], m, one) for m in range(8)]
    for v0 in range(groups):
        first = 8 * v0
        more = v0 + 1 < groups
        if more:
            ahead = [over(a[v0 + 1], first + 8 + m, one) for m in range(8)]
            spread = [under] + [
                [over(a[v], first + m, one) for m in range(8)] for v in range(v0 + 2, groups)
            ]
            rest = list(under)
        row_a, row_w = a[v0], w[v0]
        ratios = []
        for j in range(8):
            pivot = down(panel[j], j)
            reciprocal = 1.0 / pivot
            pivots = pivot if j == 0 else jnp.where(line == j, pivot, pivots)
            reciprocals = reciprocal if j == 0 else jnp.where(line == j, reciprocal, reciprocals)
            if more:
                ratios.append(rest[j] * reciprocal)
            if j < 7:
                ratio = jnp.where(line > j, panel[j] * reciprocal, 0.0)
                for m in range(j + 1, 8):
                    entry = down(panel[m], j)
                    panel[m] = panel[m] - ratio * entry
                    if more:
                        rest[m] = rest[m] - ratios[j] * entry
                row_a = row_a - ratio * down(row_a, j)
                row_w = row_w - ratio * down(row_w, j)
        result.append(row_w * lax.rsqrt(pivots))
        if more:
            following = [
                ahead[m] - add_up([ratios[j] * down(rest[j], m) for j in range(8)]) for m in range(8)
            ]
            row_a, row_w = row_a * reciprocals, row_w * reciprocals
            for j in range(7, 0, -1):
                ratio = jnp.where(line < j, panel[j] * reciprocals, 0.0)
                row_a = row_a - ratio * down(row_a, j)
                row_w = row_w - ratio * down(row_w, j)
            from_a = [down(row_a, m) for m in range(8)]
            from_w = [down(row_w, m) for m in range(8)]
            for index, v in enumerate(range(v0 + 1, groups)):
                a[v] = a[v] - add_up([spread[index][m] * from_a[m] for m in range(8)])
                w[v] = w[v] - add_up([spread[index][m] * from_w[m] for m in range(8)])
            panel = following
            if v0 + 2 < groups:
                under = [over(a[v0 + 2], first + 8 + m, one) for m in range(8)]
    return result


def split(value):
    top = value.astype(jnp.bfloat16)
    return top, (value - top.astype(jnp.float32)).astype(jnp.bfloat16)


def basis_kernel(gram_ref, stats_ref, basis_ref, high_hbm, low_hbm, factor_ref, core_ref, high, low, turned, image, inverse, sems):
    loads = [
        pltpu.make_async_copy(high_hbm, high, sems.at[0]),
        pltpu.make_async_copy(low_hbm, low, sems.at[1]),
    ]
    for load in loads:
        load.start()
    rows, rank = basis_ref.shape
    blocks = rows // BLOCK
    highest = lax.Precision.HIGHEST
    for b in range(blocks):
        turned[:, b * BLOCK:(b + 1) * BLOCK] = basis_ref[pl.ds(b * BLOCK, BLOCK), :].T
    one = stats_ref[16:24, :]

    def body(iteration, carry):
        image[...] = jnp.dot(turned[...], gram_ref[...], precision=highest, preferred_element_type=jnp.float32)
        small = dot_nt(image[...], image[...], precision=highest)
        for v, group in enumerate(inverse_factor(small, one)):
            inverse[pl.ds(8 * v, 8), :] = group
        turned[...] = jnp.dot(inverse[...], image[...], precision=highest, preferred_element_type=jnp.float32)
        return carry

    lax.fori_loop(0, ITERS, body, 0)

    constant = None
    for b in range(blocks):
        window = pl.ds(b * BLOCK, BLOCK)
        value = turned[:, window]
        factor_ref[window, :] = value.T
        value = value * stats_ref[4 + b:5 + b, :]
        image[:, window] = value
        term = value * stats_ref[8 + b:9 + b, :]
        constant = term if constant is None else constant + term
    constant = jnp.broadcast_to(jnp.sum(constant, axis=1, keepdims=True), (rank, BLOCK))
    top, rest = split(image[...])
    for load in loads:
        load.wait()
    slabs = core_ref.shape[1]
    for s in range(0, slabs, 2):
        window = pl.ds(s * BLOCK, 2 * BLOCK)
        value = jnp.dot(top, high[:, window], preferred_element_type=jnp.float32)
        value = value + jnp.dot(top, low[:, window], preferred_element_type=jnp.float32)
        value = value + jnp.dot(rest, high[:, window], preferred_element_type=jnp.float32)
        core_ref[:, s, :] = value[:, :BLOCK] + constant
        core_ref[:, s + 1, :] = value[:, BLOCK:] + constant


def basis_call(gram_matrix, stats, basis, high, low, slabs):
    rows, rank = basis.shape
    f32, bf16 = jnp.float32, jnp.bfloat16
    vmem = pl.BlockSpec(memory_space=pltpu.VMEM)
    hbm = pl.BlockSpec(memory_space=pl.ANY)
    return pl.pallas_call(
        basis_kernel,
        out_shape=(
            jax.ShapeDtypeStruct((rows, rank), f32),
            jax.ShapeDtypeStruct((rank, slabs, BLOCK), f32),
        ),
        in_specs=[vmem, vmem, vmem, hbm, hbm],
        out_specs=(vmem, vmem),
        scratch_shapes=[
            pltpu.VMEM(high.shape, bf16),
            pltpu.VMEM(low.shape, bf16),
            pltpu.VMEM((rank, rows), f32),
            pltpu.VMEM((rank, rows), f32),
            pltpu.VMEM((rank, rank), f32),
            pltpu.SemaphoreType.DMA((2,)),
        ],
    )(gram_matrix, stats, basis, high, low)


def local_step(sizes, tensor, initial_basis):
    cells = float(tensor.shape[1] * tensor.shape[2] * lax.axis_size("row") * lax.axis_size("col"))
    gram_matrix, stats, high, low = gram_call(tensor, sizes, cells)
    return basis_call(gram_matrix, stats, initial_basis, high, low, tensor.shape[1])


def solution(mesh):
    nx = CHIPS_X
    sizes = (nx, mesh.shape["row"] // nx, mesh.shape["col"] // 2)
    in_specs = (P(None, "row", "col"), P())
    out_specs = (P(), P(None, "row", "col"))
    return jax.shard_map(
        functools.partial(local_step, sizes), mesh=mesh, in_specs=in_specs, out_specs=out_specs, check_vma=False
    )
```

```python
import functools

import jax
import jax.numpy as jnp
from jax import lax
from jax.experimental import pallas as pl
from jax.experimental.pallas import tpu as pltpu
from jax.sharding import PartitionSpec as P

ITERS = 3
CHIPS_X = 4
BLOCK = 128
MESH = pl.DeviceIdType.MESH
SQUARES = ((1, 0), (2, 0), (3, 0), (0, 1), (2, 1), (3, 1), (3, 2), (2, 3))
PAIRED = (3, 7)


def ring_distance(step, extent):
    return min(step, extent - step)


def far_first(extent):
    return sorted(range(1, extent), key=lambda step: -ring_distance(step, extent))


def near_first(extent):
    return sorted(range(1, extent), key=lambda step: ring_distance(step, extent))


def add_up(terms):
    while len(terms) > 1:
        pairs = [terms[i] + terms[i + 1] for i in range(0, len(terms) - 1, 2)]
        terms = pairs + terms[2 * len(pairs):]
    return terms[0]


def split(value):
    top = value.astype(jnp.bfloat16)
    return top, (value - top.astype(jnp.float32)).astype(jnp.bfloat16)


def dot_nt(left, right, precision=None):
    return lax.dot_general(
        left, right, (((1,), (1,)), ((), ())), precision=precision, preferred_element_type=jnp.float32
    )


def gram_kernel(
    sizes, cells,
    x_hbm, gram_ref, stats_ref, high, low,
    field, local, from_core, to_x, from_x, to_z, from_z, from_y, packed,
    load_sem, core_send, core_recv, x_send, x_recv, z_send, z_recv, y_send, y_recv,
    gz_send, gz_recv, gx_send, gx_recv, gc_send, gc_recv,
):
    nx, ny, nz = sizes
    tiles_x = 64 // nx
    tiles_z = tiles_x // nz
    row, col = lax.axis_index("row"), lax.axis_index("col")
    x, y = lax.rem(row, nx), lax.div(row, nx)
    core, z = lax.rem(col, 2), lax.div(col, 2)

    def device(dx=0, dy=0, dz=0, other=False):
        to_row = lax.rem(y + dy, ny) * nx + lax.rem(x + dx, nx)
        to_col = lax.rem(z + dz, nz) * 2 + (1 - core if other else core)
        return (to_row, to_col)

    peers = [device(other=True)]
    peers += [device(dx=d) for d in range(1, nx)]
    peers += [device(dz=d) for d in range(1, nz)]
    peers += [device(dy=d) for d in range(1, ny)]
    barrier = pltpu.get_barrier_semaphore()
    for peer in peers:
        pl.semaphore_signal(barrier, inc=1, device_id=peer, device_id_type=MESH)

    def send(src, dst, send_sem, recv_sem, peer):
        copy = pltpu.make_async_remote_copy(
            src_ref=src, dst_ref=dst, send_sem=send_sem, recv_sem=recv_sem,
            device_id=peer, device_id_type=MESH,
        )
        copy.start()
        return copy

    slabs, rows = field.shape[0], field.shape[1]
    width = float(slabs * BLOCK)
    blocks = rows // BLOCK
    loads = {}
    for b in range(blocks):
        here = pl.ds(b * BLOCK, BLOCK)
        for s in range(slabs):
            loads[b, s] = pltpu.make_async_copy(x_hbm.at[here, s, :], field.at[s, here, :], load_sem.at[b, s])
            loads[b, s].start()

    below = lax.broadcasted_iota(jnp.int32, (BLOCK, BLOCK), 0)
    across = lax.broadcasted_iota(jnp.int32, (BLOCK, BLOCK), 1)
    on_diagonal = below == across

    pair = 2 * BLOCK
    mean_down, mean_over, sums, square = [], [], [], {}
    for bi in range(blocks // 2):
        for b in (2 * bi, 2 * bi + 1):
            here = pl.ds(b * BLOCK, BLOCK)
            for s in range(slabs):
                loads[b, s].wait()
            total = add_up([field[s, here, :] for s in range(slabs)])
            total = jnp.broadcast_to(jnp.sum(total, axis=1, keepdims=True), (BLOCK, BLOCK))
            mean = total * (1.0 / width)
            for s in range(slabs):
                top, rest = split(field[s, here, :] - mean)
                high[here, pl.ds(s * BLOCK, BLOCK)] = top
                low[here, pl.ds(s * BLOCK, BLOCK)] = rest
            turned = total.T
            mean_down.append(mean)
            mean_over.append(turned * (1.0 / width))
            sums.append(turned[0:1, :])
        for bj in range(bi + 1):
            left, right = pl.ds(bi * pair, pair), pl.ds(bj * pair, pair)
            value = dot_nt(high[left, :], high[right, :])
            crossed = dot_nt(high[left, :], low[right, :])
            crossed = crossed + (crossed.T if bi == bj else dot_nt(low[left, :], high[right, :]))
            value = value + crossed
            for i in range(2):
                for j in range(2):
                    r, q = 2 * bi + i, 2 * bj + j
                    if r >= q:
                        square[r, q] = value[i * BLOCK:(i + 1) * BLOCK, j * BLOCK:(j + 1) * BLOCK] + (
                            width * mean_down[r] * mean_over[q]
                        )

    def diagonal_of(block):
        return jnp.sum(jnp.where(on_diagonal, block, 0.0), axis=0, keepdims=True)

    extra = jnp.concatenate(
        sums + [diagonal_of(square[0, 0]), diagonal_of(square[2, 2]), jnp.zeros((2, BLOCK), jnp.float32)], axis=0
    )
    for index, (r, q) in enumerate(SQUARES):
        half, slot = index // 4, (index % 4) * 16
        if index in PAIRED:
            first, second = min(r, q), max(r, q)
            block = jnp.where(below > across, square[first, first], square[second, second])
        else:
            block = square[r, q]
        local[half, slot // tiles_x, pl.ds(slot % tiles_x, 16)] = block.reshape(16, 8, BLOCK)
    for half in range(2):
        for piece in range(nx):
            local[half, piece, tiles_x] = extra

    pl.semaphore_wait(barrier, len(peers))

    order_x = far_first(nx) + [0]
    partner = device(other=True)
    sent = []
    core_copies = {}
    for d in order_x:
        core_copies[d] = send(
            local.at[1 - core, lax.rem(x + d, nx)], from_core.at[d], core_send.at[d], core_recv.at[d], partner
        )
    sent += list(core_copies.values())
    x_copies = {}
    for d in order_x:
        core_copies[d].wait_recv()
        value = local[core, lax.rem(x + d, nx)] + from_core[d]
        if d == 0:
            from_x[0] = value
        else:
            to_x[d - 1] = value
            x_copies[d] = send(to_x.at[d - 1], from_x.at[d], x_send.at[d - 1], x_recv.at[d - 1], device(dx=d))
    sent += list(x_copies.values())
    for d in near_first(nx):
        x_copies[d].wait_recv()

    def x_sum(window):
        value = from_x[lax.rem(x + nx, nx), window]
        for j in range(1, nx):
            value = value + from_x[lax.rem(x + nx - j, nx), window]
        return value

    moments = x_sum(pl.ds(tiles_x, 1))
    z_copies = {}
    for d in far_first(nz) + [0]:
        value = x_sum(pl.ds(lax.rem(z + d, nz) * tiles_z, tiles_z))
        if d == 0:
            from_z[0, pl.ds(0, tiles_z)] = value
            from_z[0, pl.ds(tiles_z, 1)] = moments
        else:
            to_z[d - 1, pl.ds(0, tiles_z)] = value
            to_z[d - 1, pl.ds(tiles_z, 1)] = moments
            z_copies[d] = send(to_z.at[d - 1], from_z.at[d], z_send.at[d - 1], z_recv.at[d - 1], device(dz=d))
    sent += list(z_copies.values())
    for d in near_first(nz):
        z_copies[d].wait_recv()
    value = from_z[z]
    for j in range(1, nz):
        value = value + from_z[lax.rem(z + nz - j, nz)]
    from_y[0] = value
    y_copies = {}
    for d in far_first(ny):
        y_copies[d] = send(from_y.at[0], from_y.at[d], y_send.at[d - 1], y_recv.at[d - 1], device(dy=d))
    sent += list(y_copies.values())
    for d in near_first(ny):
        y_copies[d].wait_recv()
    value = from_y[y]
    for j in range(1, ny):
        value = value + from_y[lax.rem(y + ny - j, ny)]

    def place(dx, dz):
        tile = 64 * core + tiles_x * lax.rem(x + nx - dx, nx) + tiles_z * lax.rem(z + nz - dz, nz)
        return packed.at[pl.ds(tile, tiles_z)]

    packed[pl.ds(64 * core + tiles_x * x + tiles_z * z, tiles_z)] = value[0:tiles_z]
    extra = value[tiles_z]

    gz, gx, gc = {}, {}, {}
    mine = place(0, 0)
    for d in far_first(nz):
        gz[d] = send(mine, mine, gz_send.at[d - 1], gz_recv.at[d - 1], device(dz=d))

    def pass_on(dx, dz):
        piece = place(dx, dz)
        if dx == 0:
            for d in far_first(nx):
                gx[d, dz] = send(piece, piece, gx_send.at[d - 1, dz], gx_recv.at[d - 1, dz], device(dx=d))
        gc[dx, dz] = send(piece, piece, gc_send.at[dx, dz], gc_recv.at[dx, dz], partner)

    pass_on(0, 0)
    arrivals = [(1.0 + ring_distance(d, nz), 0, d) for d in range(1, nz)]
    arrivals += [
        ((1.0 + ring_distance(d, nz) if d else 0.0) + 1.0 + ring_distance(e, nx), e, d)
        for e in range(1, nx) for d in range(nz)
    ]
    for _, e, d in sorted(arrivals):
        if e == 0:
            gz[d].wait_recv()
        else:
            gx[e, d].wait_recv()
        pass_on(e, d)
    for copy in gc.values():
        copy.wait_recv()

    means, scales, seconds = [], [], []
    def matrix(index):
        return packed[pl.ds(16 * index, 16)].reshape(BLOCK, BLOCK)

    whole = {}
    for index, (r, q) in enumerate(SQUARES):
        block = matrix(index)
        if index in PAIRED:
            first, second = min(r, q), max(r, q)
            turned = block.T
            line = extra[4 + first // 2:5 + first // 2, :]
            whole[first, first] = jnp.where(
                below > across, block, jnp.where(below < across, turned, jnp.broadcast_to(line, (BLOCK, BLOCK)))
            )
            whole[second, second] = jnp.where(below <= across, block, turned)
        else:
            whole[r, q] = block
    for b in range(blocks):
        average = extra[b:b + 1, :] / cells
        if b % 2 == 0:
            second = extra[4 + b // 2:5 + b // 2, :]
        else:
            second = diagonal_of(whole[b, b])
        scale = 1.0 / jnp.sqrt(second / cells - average * average + 1e-05)
        stats_ref[b:b + 1, :] = average
        stats_ref[4 + b:5 + b, :] = scale
        stats_ref[8 + b:9 + b, :] = sums[b] * (1.0 / width) - average
        means.append(jnp.broadcast_to(average, (BLOCK, BLOCK)))
        scales.append(jnp.broadcast_to(scale, (BLOCK, BLOCK)))
    stats_ref[16:24, :] = jnp.ones((8, BLOCK), jnp.float32)
    means_down = [value.T for value in means]
    scales_down = [value.T for value in scales]
    for (r, q), block in whole.items():
        value = (block * (1.0 / cells) - means_down[r] * means[q]) * scales_down[r] * scales[q]
        gram_ref[pl.ds(r * BLOCK, BLOCK), pl.ds(q * BLOCK, BLOCK)] = value
        if r != q:
            gram_ref[pl.ds(q * BLOCK, BLOCK), pl.ds(r * BLOCK, BLOCK)] = value.T

    for copy in sent + list(gz.values()) + list(gx.values()) + list(gc.values()):
        copy.wait_send()


def gram_call(tensor, sizes, cells):
    nx, ny, nz = sizes
    rows, slabs, lanes = tensor.shape
    tiles_x = 64 // nx
    tiles_z = tiles_x // nz
    f32, bf16 = jnp.float32, jnp.bfloat16
    vmem = pltpu.VMEM
    dma = pltpu.SemaphoreType.DMA
    return pl.pallas_call(
        functools.partial(gram_kernel, sizes, cells),
        out_shape=(
            jax.ShapeDtypeStruct((rows, rows), f32),
            jax.ShapeDtypeStruct((24, lanes), f32),
            jax.ShapeDtypeStruct((rows, slabs * lanes), bf16),
            jax.ShapeDtypeStruct((rows, slabs * lanes), bf16),
        ),
        in_specs=[pl.BlockSpec(memory_space=pltpu.HBM)],
        out_specs=(pl.BlockSpec(memory_space=pltpu.VMEM),) * 4,
        scratch_shapes=[
            vmem((slabs, rows, lanes), f32),
            vmem((2, nx, tiles_x + 1, 8, lanes), f32),
            vmem((nx, tiles_x + 1, 8, lanes), f32),
            vmem((nx - 1, tiles_x + 1, 8, lanes), f32),
            vmem((nx, tiles_x + 1, 8, lanes), f32),
            vmem((nz - 1, tiles_z + 1, 8, lanes), f32),
            vmem((nz, tiles_z + 1, 8, lanes), f32),
            vmem((ny, tiles_z + 1, 8, lanes), f32),
            vmem((128, 8, lanes), f32),
            dma((rows // BLOCK, slabs)),
            dma((nx,)), dma((nx,)),
            dma((nx - 1,)), dma((nx - 1,)),
            dma((nz - 1,)), dma((nz - 1,)),
            dma((ny - 1,)), dma((ny - 1,)),
            dma((nz - 1,)), dma((nz - 1,)),
            dma((nx - 1, nz)), dma((nx - 1, nz)),
            dma((nx, nz)), dma((nx, nz)),
        ],
        compiler_params=pltpu.CompilerParams(
            collective_id=0, has_side_effects=True, vmem_limit_bytes=16 << 20
        ),
    )(pltpu.with_memory_space_constraint(tensor, pltpu.HBM))


def over(value, lane):
    return jnp.broadcast_to(value[:, lane:lane + 1], (8, BLOCK))


def down(value, line):
    return jnp.broadcast_to(value[line:line + 1, :], (8, BLOCK))


def eliminate(a, base, one):
    groups = len(a)
    a = list(a)
    line = lax.broadcasted_iota(jnp.int32, (8, BLOCK), 0)
    lane = lax.broadcasted_iota(jnp.int32, (8, BLOCK), 1)

    def spread(v, first):
        columns = [over(a[v], first + m) for m in range(8)]
        return [columns[0] * one, columns[1] * one] + columns[2:]

    result = []
    panel, under = spread(0, base), spread(1, base)
    for v0 in range(groups):
        first = base + 8 * v0
        more = v0 + 1 < groups
        inside = (lane >= first) & (lane < first + 8)
        if more:
            ahead = [over(a[v0 + 1], first + 8 + m) for m in range(8)]
            columns = [under] + [[over(a[v], first + m) for m in range(8)] for v in range(v0 + 2, groups)]
            rest = list(under)
        rows = jnp.where(inside, jnp.where(lane == line + first, 1.0, 0.0).astype(jnp.float32), a[v0])
        ratios, pivots = [None] * 8, {}
        for j in range(0, 8, 2):
            p, q, r = down(panel[j], j), down(panel[j], j + 1), down(panel[j + 1], j + 1)
            determinant = p * r - q * q
            inverse = 1.0 / determinant
            pi, qi, ri = p * inverse, q * inverse, r * inverse
            pivots[j] = (p, q, r, pi, qi, ri, determinant)
            if more:
                ratios[j] = rest[j] * ri - rest[j + 1] * qi
                ratios[j + 1] = rest[j + 1] * pi - rest[j] * qi
            if j < 6:
                left = jnp.where(line > j + 1, panel[j] * ri - panel[j + 1] * qi, 0.0)
                right = jnp.where(line > j + 1, panel[j + 1] * pi - panel[j] * qi, 0.0)
                for m in range(j + 2, 8):
                    upper, lower = down(panel[m], j), down(panel[m], j + 1)
                    panel[m] = panel[m] - (left * upper + right * lower)
                    if more:
                        rest[m] = rest[m] - (ratios[j] * upper + ratios[j + 1] * lower)
                rows = rows - (left * down(rows, j) + right * down(rows, j + 1))
        scaled, solved = rows, []
        for j in range(0, 8, 2):
            p, q, r, pi, qi, ri, determinant = pivots[j]
            upper, lower = down(rows, j), down(rows, j + 1)
            root = lax.rsqrt(p)
            square = root * root
            scaled = jnp.where(line == j, upper * root, scaled)
            scaled = jnp.where(
                line == j + 1, (lower - q * square * upper) * lax.rsqrt(determinant * square), scaled
            )
            solved.append((ri * upper - qi * lower, pi * lower - qi * upper))
        result.append(scaled)
        if more:
            following = [
                ahead[m] - add_up([ratios[j] * down(rest[j], m) for j in range(8)]) for m in range(8)
            ]
            change = [None] * 8
            for j in range(6, -1, -2):
                upper, lower = solved[j // 2]
                if j < 6:
                    p, q, r, pi, qi, ri, determinant = pivots[j]
                    first_sum = add_up([down(panel[m], j) * change[m] for m in range(j + 2, 8)])
                    second_sum = add_up([down(panel[m], j + 1) * change[m] for m in range(j + 2, 8)])
                    upper = upper - (ri * first_sum - qi * second_sum)
                    lower = lower - (pi * second_sum - qi * first_sum)
                change[j], change[j + 1] = upper, lower
            for index, v in enumerate(range(v0 + 1, groups)):
                a[v] = jnp.where(inside, 0.0, a[v]) - add_up([columns[index][m] * change[m] for m in range(8)])
            panel = following
            if v0 + 2 < groups:
                under = spread(v0 + 2, first + 8)
    return result


def inverse_factor(matrix, one):
    lane = lax.broadcasted_iota(jnp.int32, (8, BLOCK), 1)
    half = BLOCK // 2
    groups = [matrix[8 * v:8 * v + 8, :] for v in range(BLOCK // 8)]
    top = eliminate(groups[:8], 0, one)
    top = [jnp.where((lane < 8 * v + 8) | (lane >= half), rows, 0.0) for v, rows in enumerate(top)]
    beyond = [jnp.where(lane >= half, rows, 0.0) for rows in top]
    change = lax.dot_general(
        jnp.concatenate(beyond, axis=0), jnp.concatenate(top, axis=0), (((0,), (0,)), ((), ())),
        precision=lax.Precision.HIGHEST, preferred_element_type=jnp.float32,
    )
    bottom = [
        jnp.where(lane >= half, rows, 0.0) - change[half + 8 * v:half + 8 * v + 8, :]
        for v, rows in enumerate(groups[8:])
    ]
    bottom = eliminate(bottom, half, one)
    bottom = [jnp.where(lane < half + 8 * v + 8, rows, 0.0) for v, rows in enumerate(bottom)]
    return [jnp.where(lane < half, rows, 0.0) for rows in top] + bottom


def basis_kernel(gram_ref, stats_ref, basis_ref, high, low, factor_ref, core_ref, turned, image, inverse):
    rows, rank = basis_ref.shape
    blocks = rows // BLOCK
    highest = lax.Precision.HIGHEST
    for b in range(blocks):
        turned[:, b * BLOCK:(b + 1) * BLOCK] = basis_ref[pl.ds(b * BLOCK, BLOCK), :].T
    one = stats_ref[16:24, :]

    def body(iteration, carry):
        image[...] = jnp.dot(turned[...], gram_ref[...], precision=highest, preferred_element_type=jnp.float32)
        small = dot_nt(image[...], image[...], precision=highest)
        for v, group in enumerate(inverse_factor(small, one)):
            inverse[pl.ds(8 * v, 8), :] = group
        turned[...] = jnp.dot(inverse[...], image[...], precision=highest, preferred_element_type=jnp.float32)
        return carry

    lax.fori_loop(0, ITERS, body, 0)

    constant = None
    for b in range(blocks):
        window = pl.ds(b * BLOCK, BLOCK)
        value = turned[:, window]
        factor_ref[window, :] = value.T
        value = value * stats_ref[4 + b:5 + b, :]
        image[:, window] = value
        term = value * stats_ref[8 + b:9 + b, :]
        constant = term if constant is None else constant + term
    constant = jnp.broadcast_to(jnp.sum(constant, axis=1, keepdims=True), (rank, BLOCK))
    top, rest = split(image[...])
    slabs = core_ref.shape[1]
    for s in range(0, slabs, 2):
        window = pl.ds(s * BLOCK, 2 * BLOCK)
        value = jnp.dot(top, high[:, window], preferred_element_type=jnp.float32)
        value = value + jnp.dot(top, low[:, window], preferred_element_type=jnp.float32)
        value = value + jnp.dot(rest, high[:, window], preferred_element_type=jnp.float32)
        core_ref[:, s, :] = value[:, :BLOCK] + constant
        core_ref[:, s + 1, :] = value[:, BLOCK:] + constant


def basis_call(gram_matrix, stats, basis, high, low, slabs):
    rows, rank = basis.shape
    f32 = jnp.float32
    vmem = pl.BlockSpec(memory_space=pltpu.VMEM)
    return pl.pallas_call(
        basis_kernel,
        out_shape=(
            jax.ShapeDtypeStruct((rows, rank), f32),
            jax.ShapeDtypeStruct((rank, slabs, BLOCK), f32),
        ),
        in_specs=[vmem] * 5,
        out_specs=(vmem, vmem),
        scratch_shapes=[
            pltpu.VMEM((rank, rows), f32),
            pltpu.VMEM((rank, rows), f32),
            pltpu.VMEM((rank, rank), f32),
        ],
        compiler_params=pltpu.CompilerParams(vmem_limit_bytes=16 << 20),
    )(gram_matrix, stats, basis, high, low)


def local_step(sizes, tensor, initial_basis):
    cells = float(tensor.shape[1] * tensor.shape[2] * lax.axis_size("row") * lax.axis_size("col"))
    gram_matrix, stats, high, low = gram_call(tensor, sizes, cells)
    return basis_call(gram_matrix, stats, initial_basis, high, low, tensor.shape[1])


def solution(mesh):
    nx = CHIPS_X
    sizes = (nx, mesh.shape["row"] // nx, mesh.shape["col"] // 2)
    in_specs = (P(None, "row", "col"), P())
    out_specs = (P(), P(None, "row", "col"))
    return jax.shard_map(
        functools.partial(local_step, sizes), mesh=mesh, in_specs=in_specs, out_specs=out_specs, check_vma=False
    )
```

```python
import functools

import jax
import jax.numpy as jnp
from jax import lax
from jax.experimental import pallas as pl
from jax.experimental.pallas import tpu as pltpu
from jax.sharding import PartitionSpec as P

ITERS = 3
CHIPS_X = 4
BLOCK = 128
MESH = pl.DeviceIdType.MESH
SQUARES = ((1, 0), (2, 0), (3, 0), (0, 1), (2, 1), (3, 1), (3, 2), (2, 3))
PAIRED = (3, 7)


def ring_distance(step, extent):
    return min(step, extent - step)


def far_first(extent):
    return sorted(range(1, extent), key=lambda step: -ring_distance(step, extent))


def near_first(extent):
    return sorted(range(1, extent), key=lambda step: ring_distance(step, extent))


def add_up(terms):
    while len(terms) > 1:
        pairs = [terms[i] + terms[i + 1] for i in range(0, len(terms) - 1, 2)]
        terms = pairs + terms[2 * len(pairs):]
    return terms[0]


def split(value):
    top = value.astype(jnp.bfloat16)
    return top, (value - top.astype(jnp.float32)).astype(jnp.bfloat16)


def dot_nt(left, right, precision=None):
    return lax.dot_general(
        left, right, (((1,), (1,)), ((), ())), precision=precision, preferred_element_type=jnp.float32
    )


def gram_kernel(
    sizes, cells,
    x_hbm, gram_ref, stats_ref, high, low,
    field, local, from_core, to_x, from_x, to_z, from_z, from_y, packed,
    load_sem, core_send, core_recv, x_send, x_recv, z_send, z_recv, y_send, y_recv,
    gz_send, gz_recv, gx_send, gx_recv, gc_send, gc_recv,
):
    nx, ny, nz = sizes
    tiles_x = 64 // nx
    tiles_z = tiles_x // nz
    row, col = lax.axis_index("row"), lax.axis_index("col")
    x, y = lax.rem(row, nx), lax.div(row, nx)
    core, z = lax.rem(col, 2), lax.div(col, 2)

    def device(dx=0, dy=0, dz=0, other=False):
        to_row = lax.rem(y + dy, ny) * nx + lax.rem(x + dx, nx)
        to_col = lax.rem(z + dz, nz) * 2 + (1 - core if other else core)
        return (to_row, to_col)

    peers = [device(other=True)]
    peers += [device(dx=d) for d in range(1, nx)]
    peers += [device(dz=d) for d in range(1, nz)]
    peers += [device(dy=d) for d in range(1, ny)]
    barrier = pltpu.get_barrier_semaphore()
    for peer in peers:
        pl.semaphore_signal(barrier, inc=1, device_id=peer, device_id_type=MESH)

    def send(src, dst, send_sem, recv_sem, peer):
        copy = pltpu.make_async_remote_copy(
            src_ref=src, dst_ref=dst, send_sem=send_sem, recv_sem=recv_sem,
            device_id=peer, device_id_type=MESH,
        )
        copy.start()
        return copy

    slabs, rows = field.shape[0], field.shape[1]
    width = float(slabs * BLOCK)
    blocks = rows // BLOCK
    loads = {}
    for b in range(blocks):
        here = pl.ds(b * BLOCK, BLOCK)
        for s in range(slabs):
            loads[b, s] = pltpu.make_async_copy(x_hbm.at[here, s, :], field.at[s, here, :], load_sem.at[b, s])
            loads[b, s].start()

    below = lax.broadcasted_iota(jnp.int32, (BLOCK, BLOCK), 0)
    across = lax.broadcasted_iota(jnp.int32, (BLOCK, BLOCK), 1)
    on_diagonal = below == across

    pair = 2 * BLOCK
    mean_down, mean_over, sums, square = [], [], [], {}
    for bi in range(blocks // 2):
        for b in (2 * bi, 2 * bi + 1):
            here = pl.ds(b * BLOCK, BLOCK)
            for s in range(slabs):
                loads[b, s].wait()
            total = add_up([field[s, here, :] for s in range(slabs)])
            total = jnp.broadcast_to(jnp.sum(total, axis=1, keepdims=True), (BLOCK, BLOCK))
            mean = total * (1.0 / width)
            for s in range(slabs):
                top, rest = split(field[s, here, :] - mean)
                high[here, pl.ds(s * BLOCK, BLOCK)] = top
                low[here, pl.ds(s * BLOCK, BLOCK)] = rest
            turned = total.T
            mean_down.append(mean)
            mean_over.append(turned * (1.0 / width))
            sums.append(turned[0:1, :])
        for bj in range(bi + 1):
            left, right = pl.ds(bi * pair, pair), pl.ds(bj * pair, pair)
            value = dot_nt(high[left, :], high[right, :])
            crossed = dot_nt(high[left, :], low[right, :])
            crossed = crossed + (crossed.T if bi == bj else dot_nt(low[left, :], high[right, :]))
            value = value + crossed
            for i in range(2):
                for j in range(2):
                    r, q = 2 * bi + i, 2 * bj + j
                    if r >= q:
                        square[r, q] = value[i * BLOCK:(i + 1) * BLOCK, j * BLOCK:(j + 1) * BLOCK] + (
                            width * mean_down[r] * mean_over[q]
                        )

    def diagonal_of(block):
        return jnp.sum(jnp.where(on_diagonal, block, 0.0), axis=0, keepdims=True)

    extra = jnp.concatenate(
        sums + [diagonal_of(square[0, 0]), diagonal_of(square[2, 2]), jnp.zeros((2, BLOCK), jnp.float32)], axis=0
    )
    for index, (r, q) in enumerate(SQUARES):
        half, slot = index // 4, (index % 4) * 16
        if index in PAIRED:
            first, second = min(r, q), max(r, q)
            block = jnp.where(below > across, square[first, first], square[second, second])
        else:
            block = square[r, q]
        local[half, slot // tiles_x, pl.ds(slot % tiles_x, 16)] = block.reshape(16, 8, BLOCK)
    for half in range(2):
        for piece in range(nx):
            local[half, piece, tiles_x] = extra

    pl.semaphore_wait(barrier, len(peers))

    order_x = far_first(nx) + [0]
    partner = device(other=True)
    sent = []
    whole_half = send(local.at[1 - core], from_core, core_send.at[0], core_recv.at[0], partner)
    sent.append(whole_half)
    whole_half.wait_recv()
    x_copies = {}
    for d in order_x:
        value = local[core, lax.rem(x + d, nx)] + from_core[lax.rem(x + d, nx)]
        if d == 0:
            from_x[0] = value
        else:
            to_x[d - 1] = value
            x_copies[d] = send(to_x.at[d - 1], from_x.at[d], x_send.at[d - 1], x_recv.at[d - 1], device(dx=d))
    sent += list(x_copies.values())
    for d in near_first(nx):
        x_copies[d].wait_recv()

    def x_sum(window):
        value = from_x[lax.rem(x + nx, nx), window]
        for j in range(1, nx):
            value = value + from_x[lax.rem(x + nx - j, nx), window]
        return value

    moments = x_sum(pl.ds(tiles_x, 1))
    z_copies = {}
    for d in far_first(nz) + [0]:
        value = x_sum(pl.ds(lax.rem(z + d, nz) * tiles_z, tiles_z))
        if d == 0:
            from_z[0, pl.ds(0, tiles_z)] = value
            from_z[0, pl.ds(tiles_z, 1)] = moments
        else:
            to_z[d - 1, pl.ds(0, tiles_z)] = value
            to_z[d - 1, pl.ds(tiles_z, 1)] = moments
            z_copies[d] = send(to_z.at[d - 1], from_z.at[d], z_send.at[d - 1], z_recv.at[d - 1], device(dz=d))
    sent += list(z_copies.values())
    for d in near_first(nz):
        z_copies[d].wait_recv()
    value = from_z[z]
    for j in range(1, nz):
        value = value + from_z[lax.rem(z + nz - j, nz)]
    from_y[0] = value
    y_copies = {}
    for d in far_first(ny):
        y_copies[d] = send(from_y.at[0], from_y.at[d], y_send.at[d - 1], y_recv.at[d - 1], device(dy=d))
    sent += list(y_copies.values())
    for d in near_first(ny):
        y_copies[d].wait_recv()
    value = from_y[y]
    for j in range(1, ny):
        value = value + from_y[lax.rem(y + ny - j, ny)]

    def place(dx, dz):
        tile = 64 * core + tiles_x * lax.rem(x + nx - dx, nx) + tiles_z * lax.rem(z + nz - dz, nz)
        return packed.at[pl.ds(tile, tiles_z)]

    packed[pl.ds(64 * core + tiles_x * x + tiles_z * z, tiles_z)] = value[0:tiles_z]
    extra = value[tiles_z]

    gz, gx, gc = {}, {}, {}
    mine = place(0, 0)
    for d in far_first(nz):
        gz[d] = send(mine, mine, gz_send.at[d - 1], gz_recv.at[d - 1], device(dz=d))

    for d in near_first(nz):
        gz[d].wait_recv()
    def square_at(dx):
        return packed.at[pl.ds(64 * core + tiles_x * lax.rem(x + nx - dx, nx), tiles_x)]
    for d in far_first(nx):
        gx[d] = send(square_at(0), square_at(0), gx_send.at[d - 1, 0], gx_recv.at[d - 1, 0], device(dx=d))
    gc[0] = send(square_at(0), square_at(0), gc_send.at[0, 0], gc_recv.at[0, 0], partner)
    for d in near_first(nx):
        gx[d].wait_recv()
        gc[d] = send(square_at(d), square_at(d), gc_send.at[d, 0], gc_recv.at[d, 0], partner)
    for copy in gc.values():
        copy.wait_recv()

    means, scales, seconds = [], [], []
    def matrix(index):
        return packed[pl.ds(16 * index, 16)].reshape(BLOCK, BLOCK)

    whole = {}
    for index, (r, q) in enumerate(SQUARES):
        block = matrix(index)
        if index in PAIRED:
            first, second = min(r, q), max(r, q)
            turned = block.T
            line = extra[4 + first // 2:5 + first // 2, :]
            whole[first, first] = jnp.where(
                below > across, block, jnp.where(below < across, turned, jnp.broadcast_to(line, (BLOCK, BLOCK)))
            )
            whole[second, second] = jnp.where(below <= across, block, turned)
        else:
            whole[r, q] = block
    for b in range(blocks):
        average = extra[b:b + 1, :] / cells
        if b % 2 == 0:
            second = extra[4 + b // 2:5 + b // 2, :]
        else:
            second = diagonal_of(whole[b, b])
        scale = 1.0 / jnp.sqrt(second / cells - average * average + 1e-05)
        stats_ref[b:b + 1, :] = average
        stats_ref[4 + b:5 + b, :] = scale
        stats_ref[8 + b:9 + b, :] = sums[b] * (1.0 / width) - average
        means.append(jnp.broadcast_to(average, (BLOCK, BLOCK)))
        scales.append(jnp.broadcast_to(scale, (BLOCK, BLOCK)))
    stats_ref[16:24, :] = jnp.ones((8, BLOCK), jnp.float32)
    means_down = [value.T for value in means]
    scales_down = [value.T for value in scales]
    for (r, q), block in whole.items():
        value = (block * (1.0 / cells) - means_down[r] * means[q]) * scales_down[r] * scales[q]
        gram_ref[pl.ds(r * BLOCK, BLOCK), pl.ds(q * BLOCK, BLOCK)] = value
        if r != q:
            gram_ref[pl.ds(q * BLOCK, BLOCK), pl.ds(r * BLOCK, BLOCK)] = value.T

    for copy in sent + list(gz.values()) + list(gx.values()) + list(gc.values()):
        copy.wait_send()


def gram_call(tensor, sizes, cells):
    nx, ny, nz = sizes
    rows, slabs, lanes = tensor.shape
    tiles_x = 64 // nx
    tiles_z = tiles_x // nz
    f32, bf16 = jnp.float32, jnp.bfloat16
    vmem = pltpu.VMEM
    dma = pltpu.SemaphoreType.DMA
    return pl.pallas_call(
        functools.partial(gram_kernel, sizes, cells),
        out_shape=(
            jax.ShapeDtypeStruct((rows, rows), f32),
            jax.ShapeDtypeStruct((24, lanes), f32),
            jax.ShapeDtypeStruct((rows, slabs * lanes), bf16),
            jax.ShapeDtypeStruct((rows, slabs * lanes), bf16),
        ),
        in_specs=[pl.BlockSpec(memory_space=pltpu.HBM)],
        out_specs=(pl.BlockSpec(memory_space=pltpu.VMEM),) * 4,
        scratch_shapes=[
            vmem((slabs, rows, lanes), f32),
            vmem((2, nx, tiles_x + 1, 8, lanes), f32),
            vmem((nx, tiles_x + 1, 8, lanes), f32),
            vmem((nx - 1, tiles_x + 1, 8, lanes), f32),
            vmem((nx, tiles_x + 1, 8, lanes), f32),
            vmem((nz - 1, tiles_z + 1, 8, lanes), f32),
            vmem((nz, tiles_z + 1, 8, lanes), f32),
            vmem((ny, tiles_z + 1, 8, lanes), f32),
            vmem((128, 8, lanes), f32),
            dma((rows // BLOCK, slabs)),
            dma((nx,)), dma((nx,)),
            dma((nx - 1,)), dma((nx - 1,)),
            dma((nz - 1,)), dma((nz - 1,)),
            dma((ny - 1,)), dma((ny - 1,)),
            dma((nz - 1,)), dma((nz - 1,)),
            dma((nx - 1, nz)), dma((nx - 1, nz)),
            dma((nx, nz)), dma((nx, nz)),
        ],
        compiler_params=pltpu.CompilerParams(
            collective_id=0, has_side_effects=True, vmem_limit_bytes=16 << 20
        ),
    )(pltpu.with_memory_space_constraint(tensor, pltpu.HBM))


def over(value, lane):
    return jnp.broadcast_to(value[:, lane:lane + 1], (8, BLOCK))


def down(value, line):
    return jnp.broadcast_to(value[line:line + 1, :], (8, BLOCK))


def eliminate(a, base, one, aside=()):
    groups = len(a)
    a = list(a)
    line = lax.broadcasted_iota(jnp.int32, (8, BLOCK), 0)
    lane = lax.broadcasted_iota(jnp.int32, (8, BLOCK), 1)

    def spread(v, first):
        columns = [over(a[v], first + m) for m in range(8)]
        return [columns[0] * one, columns[1] * one] + columns[2:]

    result = []
    panel, under = spread(0, base), spread(1, base)
    for v0 in range(groups):
        if v0 < len(aside):
            aside[v0]()
        first = base + 8 * v0
        more = v0 + 1 < groups
        inside = (lane >= first) & (lane < first + 8)
        if more:
            ahead = [over(a[v0 + 1], first + 8 + m) for m in range(8)]
            columns = [under] + [[over(a[v], first + m) for m in range(8)] for v in range(v0 + 2, groups)]
            rest = list(under)
        rows = jnp.where(inside, jnp.where(lane == line + first, 1.0, 0.0).astype(jnp.float32), a[v0])
        ratios, pivots = [None] * 8, {}
        for j in range(0, 8, 2):
            p, q, r = down(panel[j], j), down(panel[j], j + 1), down(panel[j + 1], j + 1)
            determinant = p * r - q * q
            inverse = 1.0 / determinant
            pi, qi, ri = p * inverse, q * inverse, r * inverse
            pivots[j] = (p, q, r, pi, qi, ri, determinant)
            if more:
                ratios[j] = rest[j] * ri - rest[j + 1] * qi
                ratios[j + 1] = rest[j + 1] * pi - rest[j] * qi
            if j < 6:
                left = jnp.where(line > j + 1, panel[j] * ri - panel[j + 1] * qi, 0.0)
                right = jnp.where(line > j + 1, panel[j + 1] * pi - panel[j] * qi, 0.0)
                for m in range(j + 2, 8):
                    upper, lower = down(panel[m], j), down(panel[m], j + 1)
                    panel[m] = panel[m] - (left * upper + right * lower)
                    if more:
                        rest[m] = rest[m] - (ratios[j] * upper + ratios[j + 1] * lower)
                rows = rows - (left * down(rows, j) + right * down(rows, j + 1))
        scaled, solved = rows, []
        for j in range(0, 8, 2):
            p, q, r, pi, qi, ri, determinant = pivots[j]
            upper, lower = down(rows, j), down(rows, j + 1)
            root = lax.rsqrt(p)
            square = root * root
            scaled = jnp.where(line == j, upper * root, scaled)
            scaled = jnp.where(
                line == j + 1, (lower - q * square * upper) * lax.rsqrt(determinant * square), scaled
            )
            solved.append((ri * upper - qi * lower, pi * lower - qi * upper))
        result.append(scaled)
        if more:
            following = [
                ahead[m] - add_up([ratios[j] * down(rest[j], m) for j in range(8)]) for m in range(8)
            ]
            change = [None] * 8
            for j in range(6, -1, -2):
                upper, lower = solved[j // 2]
                if j < 6:
                    p, q, r, pi, qi, ri, determinant = pivots[j]
                    first_sum = add_up([down(panel[m], j) * change[m] for m in range(j + 2, 8)])
                    second_sum = add_up([down(panel[m], j + 1) * change[m] for m in range(j + 2, 8)])
                    upper = upper - (ri * first_sum - qi * second_sum)
                    lower = lower - (pi * second_sum - qi * first_sum)
                change[j], change[j + 1] = upper, lower
            for index, v in enumerate(range(v0 + 1, groups)):
                a[v] = jnp.where(inside, 0.0, a[v]) - add_up([columns[index][m] * change[m] for m in range(8)])
            panel = following
            if v0 + 2 < groups:
                under = spread(v0 + 2, first + 8)
    return result


def inverse_factor(matrix, one, aside=()):
    lane = lax.broadcasted_iota(jnp.int32, (8, BLOCK), 1)
    half = BLOCK // 2
    groups = [matrix[8 * v:8 * v + 8, :] for v in range(BLOCK // 8)]
    top = eliminate(groups[:8], 0, one, aside[:8])
    top = [jnp.where((lane < 8 * v + 8) | (lane >= half), rows, 0.0) for v, rows in enumerate(top)]
    beyond = [jnp.where(lane >= half, rows, 0.0) for rows in top]
    change = lax.dot_general(
        jnp.concatenate(beyond, axis=0), jnp.concatenate(top, axis=0), (((0,), (0,)), ((), ())),
        precision=lax.Precision.HIGHEST, preferred_element_type=jnp.float32,
    )
    bottom = [
        jnp.where(lane >= half, rows, 0.0) - change[half + 8 * v:half + 8 * v + 8, :]
        for v, rows in enumerate(groups[8:])
    ]
    bottom = eliminate(bottom, half, one, aside[8:])
    bottom = [jnp.where(lane < half + 8 * v + 8, rows, 0.0) for v, rows in enumerate(bottom)]
    return [jnp.where(lane < half, rows, 0.0) for rows in top] + bottom


def basis_kernel(gram_ref, stats_ref, basis_ref, high, low, factor_ref, core_ref, turned, image, inverse):
    rows, rank = basis_ref.shape
    blocks = rows // BLOCK
    highest = lax.Precision.HIGHEST
    for b in range(blocks):
        turned[:, b * BLOCK:(b + 1) * BLOCK] = basis_ref[pl.ds(b * BLOCK, BLOCK), :].T
    one = stats_ref[16:24, :]

    def orthonormal(target, aside=()):
        small = dot_nt(image[...], image[...], precision=highest)
        for v, group in enumerate(inverse_factor(small, one, aside)):
            inverse[pl.ds(8 * v, 8), :] = group
        return jnp.dot(inverse[...], target[...], precision=highest, preferred_element_type=jnp.float32)

    def body(iteration, carry):
        def chunk(part):
            window = pl.ds(256 * part, 256)
            turned[:, window] = jnp.dot(
                image[...], gram_ref[:, window], precision=highest, preferred_element_type=jnp.float32
            )

        todo = [functools.partial(chunk, part) for part in range(2)]
        image[...] = orthonormal(turned, [todo[v // 8] if v % 8 == 0 else (lambda: None) for v in range(16)])
        return carry

    image[...] = jnp.dot(turned[...], gram_ref[...], precision=highest, preferred_element_type=jnp.float32)
    lax.fori_loop(0, ITERS - 1, body, 0)
    turned[...] = orthonormal(image)

    constant = None
    for b in range(blocks):
        window = pl.ds(b * BLOCK, BLOCK)
        value = turned[:, window]
        factor_ref[window, :] = value.T
        value = value * stats_ref[4 + b:5 + b, :]
        image[:, window] = value
        term = value * stats_ref[8 + b:9 + b, :]
        constant = term if constant is None else constant + term
    constant = jnp.broadcast_to(jnp.sum(constant, axis=1, keepdims=True), (rank, BLOCK))
    top, rest = split(image[...])
    slabs = core_ref.shape[1]
    for s in range(0, slabs, 2):
        window = pl.ds(s * BLOCK, 2 * BLOCK)
        value = jnp.dot(top, high[:, window], preferred_element_type=jnp.float32)
        value = value + jnp.dot(top, low[:, window], preferred_element_type=jnp.float32)
        value = value + jnp.dot(rest, high[:, window], preferred_element_type=jnp.float32)
        core_ref[:, s, :] = value[:, :BLOCK] + constant
        core_ref[:, s + 1, :] = value[:, BLOCK:] + constant


def basis_call(gram_matrix, stats, basis, high, low, slabs):
    rows, rank = basis.shape
    f32 = jnp.float32
    vmem = pl.BlockSpec(memory_space=pltpu.VMEM)
    return pl.pallas_call(
        basis_kernel,
        out_shape=(
            jax.ShapeDtypeStruct((rows, rank), f32),
            jax.ShapeDtypeStruct((rank, slabs, BLOCK), f32),
        ),
        in_specs=[vmem] * 5,
        out_specs=(vmem, vmem),
        scratch_shapes=[
            pltpu.VMEM((rank, rows), f32),
            pltpu.VMEM((rank, rows), f32),
            pltpu.VMEM((rank, rank), f32),
        ],
        compiler_params=pltpu.CompilerParams(vmem_limit_bytes=16 << 20),
    )(gram_matrix, stats, basis, high, low)


def local_step(sizes, tensor, initial_basis):
    cells = float(tensor.shape[1] * tensor.shape[2] * lax.axis_size("row") * lax.axis_size("col"))
    gram_matrix, stats, high, low = gram_call(tensor, sizes, cells)
    return basis_call(gram_matrix, stats, initial_basis, high, low, tensor.shape[1])


def solution(mesh):
    nx = CHIPS_X
    sizes = (nx, mesh.shape["row"] // nx, mesh.shape["col"] // 2)
    in_specs = (P(None, "row", "col"), P())
    out_specs = (P(), P(None, "row", "col"))
    return jax.shard_map(
        functools.partial(local_step, sizes), mesh=mesh, in_specs=in_specs, out_specs=out_specs, check_vma=False
    )
```

```python
import functools

import jax
import jax.numpy as jnp
from jax import lax
from jax.experimental import pallas as pl
from jax.experimental.pallas import tpu as pltpu
from jax.sharding import PartitionSpec as P

ITERS = 3
CHIPS_X = 4
BLOCK = 128
MESH = pl.DeviceIdType.MESH
SQUARES = ((1, 0), (2, 0), (3, 0), (0, 1), (2, 1), (3, 1), (3, 2), (2, 3))
PAIRED = (3, 7)


def ring_distance(step, extent):
    return min(step, extent - step)


def far_first(extent):
    return sorted(range(1, extent), key=lambda step: -ring_distance(step, extent))


def near_first(extent):
    return sorted(range(1, extent), key=lambda step: ring_distance(step, extent))


def add_up(terms):
    while len(terms) > 1:
        pairs = [terms[i] + terms[i + 1] for i in range(0, len(terms) - 1, 2)]
        terms = pairs + terms[2 * len(pairs):]
    return terms[0]


def split(value):
    top = value.astype(jnp.bfloat16)
    return top, (value - top.astype(jnp.float32)).astype(jnp.bfloat16)


def dot_nt(left, right, precision=None):
    return lax.dot_general(
        left, right, (((1,), (1,)), ((), ())), precision=precision, preferred_element_type=jnp.float32
    )


def gram_kernel(
    sizes, cells,
    x_hbm, gram_ref, stats_ref, high, low,
    field, local, from_core, to_x, from_x, to_z, from_z, from_y, packed, across_ref, down_ref,
    load_sem, core_send, core_recv, x_send, x_recv, z_send, z_recv, y_send, y_recv,
    gz_send, gz_recv, gx_send, gx_recv, gc_send, gc_recv,
):
    nx, ny, nz = sizes
    tiles_x = 64 // nx
    tiles_z = tiles_x // nz
    row, col = lax.axis_index("row"), lax.axis_index("col")
    x, y = lax.rem(row, nx), lax.div(row, nx)
    core, z = lax.rem(col, 2), lax.div(col, 2)

    def device(dx=0, dy=0, dz=0, other=False):
        to_row = lax.rem(y + dy, ny) * nx + lax.rem(x + dx, nx)
        to_col = lax.rem(z + dz, nz) * 2 + (1 - core if other else core)
        return (to_row, to_col)

    reach = [(-ring_distance(d, nz), device(dz=d)) for d in range(1, nz)]
    reach += [(-ring_distance(d, ny), device(dy=d)) for d in range(1, ny)]
    reach += [(-ring_distance(d, nx), device(dx=d)) for d in range(1, nx)]
    peers = [peer for _, peer in sorted(reach, key=lambda entry: entry[0])] + [device(other=True)]
    barrier = pltpu.get_barrier_semaphore()
    for peer in peers:
        pl.semaphore_signal(barrier, inc=1, device_id=peer, device_id_type=MESH)

    def send(src, dst, send_sem, recv_sem, peer):
        copy = pltpu.make_async_remote_copy(
            src_ref=src, dst_ref=dst, send_sem=send_sem, recv_sem=recv_sem,
            device_id=peer, device_id_type=MESH,
        )
        copy.start()
        return copy

    slabs, rows = field.shape[0], field.shape[1]
    width = float(slabs * BLOCK)
    blocks = rows // BLOCK
    loads = {}
    for b in range(blocks):
        here = pl.ds(b * BLOCK, BLOCK)
        for s in range(slabs):
            loads[b, s] = pltpu.make_async_copy(x_hbm.at[here, s, :], field.at[s, here, :], load_sem.at[b, s])
            loads[b, s].start()

    below = lax.broadcasted_iota(jnp.int32, (BLOCK, BLOCK), 0)
    across = lax.broadcasted_iota(jnp.int32, (BLOCK, BLOCK), 1)
    on_diagonal = below == across

    pair = 2 * BLOCK
    mean_down, mean_over, sums, square = [], [], [], {}
    for bi in range(blocks // 2):
        for b in (2 * bi, 2 * bi + 1):
            here = pl.ds(b * BLOCK, BLOCK)
            for s in range(slabs):
                loads[b, s].wait()
            total = add_up([field[s, here, :] for s in range(slabs)])
            total = jnp.broadcast_to(jnp.sum(total, axis=1, keepdims=True), (BLOCK, BLOCK))
            mean = total * (1.0 / width)
            for s in range(slabs):
                top, rest = split(field[s, here, :] - mean)
                high[here, pl.ds(s * BLOCK, BLOCK)] = top
                low[here, pl.ds(s * BLOCK, BLOCK)] = rest
            turned = total.T
            mean_down.append(mean)
            mean_over.append(turned * (1.0 / width))
            sums.append(turned[0:1, :])
        for bj in range(bi + 1):
            left, right = pl.ds(bi * pair, pair), pl.ds(bj * pair, pair)
            value = dot_nt(high[left, :], high[right, :])
            crossed = dot_nt(high[left, :], low[right, :])
            crossed = crossed + (crossed.T if bi == bj else dot_nt(low[left, :], high[right, :]))
            value = value + crossed
            for i in range(2):
                for j in range(2):
                    r, q = 2 * bi + i, 2 * bj + j
                    if r >= q:
                        square[r, q] = value[i * BLOCK:(i + 1) * BLOCK, j * BLOCK:(j + 1) * BLOCK] + (
                            width * mean_down[r] * mean_over[q]
                        )

    def diagonal_of(block):
        return jnp.sum(jnp.where(on_diagonal, block, 0.0), axis=0, keepdims=True)

    extra = jnp.concatenate(
        sums + [diagonal_of(square[b, b]) for b in range(blocks)], axis=0
    )
    for index, (r, q) in enumerate(SQUARES):
        half, slot = index // 4, (index % 4) * 16
        if index in PAIRED:
            first, second = min(r, q), max(r, q)
            block = jnp.where(below > across, square[first, first], square[second, second])
        else:
            block = square[r, q]
        local[half, slot // tiles_x, pl.ds(slot % tiles_x, 16)] = block.reshape(16, 8, BLOCK)
    for half in range(2):
        for piece in range(nx):
            local[half, piece, tiles_x] = extra

    pl.semaphore_wait(barrier, len(peers))

    order_x = far_first(nx) + [0]
    partner = device(other=True)
    sent = []
    whole_half = send(local.at[1 - core], from_core, core_send.at[0], core_recv.at[0], partner)
    sent.append(whole_half)
    whole_half.wait_recv()
    x_copies = {}
    for d in order_x:
        value = local[core, lax.rem(x + d, nx)] + from_core[lax.rem(x + d, nx)]
        if d == 0:
            from_x[0] = value
        else:
            to_x[d - 1] = value
            x_copies[d] = send(to_x.at[d - 1], from_x.at[d], x_send.at[d - 1], x_recv.at[d - 1], device(dx=d))
    sent += list(x_copies.values())
    for d in near_first(nx):
        x_copies[d].wait_recv()

    def x_sum(window):
        value = from_x[lax.rem(x + nx, nx), window]
        for j in range(1, nx):
            value = value + from_x[lax.rem(x + nx - j, nx), window]
        return value

    moments = x_sum(pl.ds(tiles_x, 1))
    z_copies = {}
    for d in far_first(nz) + [0]:
        value = x_sum(pl.ds(lax.rem(z + d, nz) * tiles_z, tiles_z))
        if d == 0:
            from_z[0, pl.ds(0, tiles_z)] = value
            from_z[0, pl.ds(tiles_z, 1)] = moments
        else:
            to_z[d - 1, pl.ds(0, tiles_z)] = value
            to_z[d - 1, pl.ds(tiles_z, 1)] = moments
            z_copies[d] = send(to_z.at[d - 1], from_z.at[d], z_send.at[d - 1], z_recv.at[d - 1], device(dz=d))
    sent += list(z_copies.values())
    for d in near_first(nz):
        z_copies[d].wait_recv()
    value = from_z[z]
    for j in range(1, nz):
        value = value + from_z[lax.rem(z + nz - j, nz)]
    from_y[0] = value
    y_copies = {}
    for d in far_first(ny):
        y_copies[d] = send(from_y.at[0], from_y.at[d], y_send.at[d - 1], y_recv.at[d - 1], device(dy=d))
    sent += list(y_copies.values())
    for d in near_first(ny):
        y_copies[d].wait_recv()
    value = from_y[y]
    for j in range(1, ny):
        value = value + from_y[lax.rem(y + ny - j, ny)]

    def place(dx, dz):
        tile = 64 * core + tiles_x * lax.rem(x + nx - dx, nx) + tiles_z * lax.rem(z + nz - dz, nz)
        return packed.at[pl.ds(tile, tiles_z)]

    packed[pl.ds(64 * core + tiles_x * x + tiles_z * z, tiles_z)] = value[0:tiles_z]
    extra = value[tiles_z]

    gz, gx, gc = {}, {}, {}
    mine = place(0, 0)
    for d in far_first(nz):
        gz[d] = send(mine, mine, gz_send.at[d - 1], gz_recv.at[d - 1], device(dz=d))

    def turn(line):
        return jnp.broadcast_to(line, (BLOCK, BLOCK)).T

    for b in range(blocks):
        average = extra[b:b + 1, :] / cells
        scale = 1.0 / jnp.sqrt(extra[4 + b:5 + b, :] / cells - average * average + 1e-05)
        stats_ref[b:b + 1, :] = average
        stats_ref[4 + b:5 + b, :] = scale
        stats_ref[8 + b:9 + b, :] = sums[b] * (1.0 / width) - average
        across_ref[0, b] = jnp.broadcast_to(scale * (1.0 / cells), (8, BLOCK))
        across_ref[1, b] = jnp.broadcast_to(scale * average, (8, BLOCK))
        across_ref[2, b] = jnp.broadcast_to(extra[4 + b:5 + b, :], (8, BLOCK))
        down_ref[0, b] = turn(scale)
        down_ref[1, b] = turn(scale * average)
    stats_ref[16:24, :] = jnp.ones((8, BLOCK), jnp.float32)

    for d in near_first(nz):
        gz[d].wait_recv()

    def square_at(dx):
        return packed.at[pl.ds(64 * core + tiles_x * lax.rem(x + nx - dx, nx), tiles_x)]

    for d in far_first(nx):
        gx[d] = send(square_at(0), square_at(0), gx_send.at[d - 1], gx_recv.at[d - 1], device(dx=d))
    gc[0] = send(square_at(0), square_at(0), gc_send.at[0], gc_recv.at[0], partner)
    for d in near_first(nx):
        gx[d].wait_recv()
        gc[d] = send(square_at(d), square_at(d), gc_send.at[d], gc_recv.at[d], partner)

    def spot(block_index):
        return pl.ds(pl.multiple_of(block_index * BLOCK, BLOCK), BLOCK)

    def put(block, r, q, mirror):
        value = block * (down_ref[0, r] * across_ref[0, q][0:1, :]) - down_ref[1, r] * across_ref[1, q][0:1, :]
        gram_ref[spot(r), spot(q)] = value
        if mirror:
            gram_ref[spot(q), spot(r)] = value.T

    def unpack(half):
        for slot in range(4):
            block = packed[pl.ds(64 * half + 16 * slot, 16)].reshape(BLOCK, BLOCK)
            (r, q), (later_r, later_q) = SQUARES[slot], SQUARES[4 + slot]
            r, q = r + half * (later_r - r), q + half * (later_q - q)
            if slot in PAIRED:
                turned = block.T
                line = jnp.broadcast_to(across_ref[2, r][0:1, :], (BLOCK, BLOCK))
                put(jnp.where(below > across, block, jnp.where(below < across, turned, line)), r, r, False)
                put(jnp.where(below <= across, block, turned), q, q, False)
            else:
                put(block, r, q, True)

    unpack(core)
    for copy in gc.values():
        copy.wait_recv()
    unpack(1 - core)

    for copy in sent + list(gz.values()) + list(gx.values()) + list(gc.values()):
        copy.wait_send()


def gram_call(tensor, sizes, cells):
    nx, ny, nz = sizes
    rows, slabs, lanes = tensor.shape
    tiles_x = 64 // nx
    tiles_z = tiles_x // nz
    f32, bf16 = jnp.float32, jnp.bfloat16
    vmem = pltpu.VMEM
    dma = pltpu.SemaphoreType.DMA
    return pl.pallas_call(
        functools.partial(gram_kernel, sizes, cells),
        out_shape=(
            jax.ShapeDtypeStruct((rows, rows), f32),
            jax.ShapeDtypeStruct((24, lanes), f32),
            jax.ShapeDtypeStruct((rows, slabs * lanes), bf16),
            jax.ShapeDtypeStruct((rows, slabs * lanes), bf16),
        ),
        in_specs=[pl.BlockSpec(memory_space=pltpu.HBM)],
        out_specs=(pl.BlockSpec(memory_space=pltpu.VMEM),) * 4,
        scratch_shapes=[
            vmem((slabs, rows, lanes), f32),
            vmem((2, nx, tiles_x + 1, 8, lanes), f32),
            vmem((nx, tiles_x + 1, 8, lanes), f32),
            vmem((nx - 1, tiles_x + 1, 8, lanes), f32),
            vmem((nx, tiles_x + 1, 8, lanes), f32),
            vmem((nz - 1, tiles_z + 1, 8, lanes), f32),
            vmem((nz, tiles_z + 1, 8, lanes), f32),
            vmem((ny, tiles_z + 1, 8, lanes), f32),
            vmem((128, 8, lanes), f32),
            vmem((3, rows // BLOCK, 8, lanes), f32),
            vmem((2, rows // BLOCK, BLOCK, lanes), f32),
            dma((rows // BLOCK, slabs)),
            dma((nx,)), dma((nx,)),
            dma((nx - 1,)), dma((nx - 1,)),
            dma((nz - 1,)), dma((nz - 1,)),
            dma((ny - 1,)), dma((ny - 1,)),
            dma((nz - 1,)), dma((nz - 1,)),
            dma((nx - 1,)), dma((nx - 1,)),
            dma((nx,)), dma((nx,)),
        ],
        compiler_params=pltpu.CompilerParams(
            collective_id=0, has_side_effects=True, vmem_limit_bytes=16 << 20
        ),
    )(pltpu.with_memory_space_constraint(tensor, pltpu.HBM))


def over(value, lane):
    return jnp.broadcast_to(value[:, lane:lane + 1], (8, BLOCK))


def down(value, line):
    return jnp.broadcast_to(value[line:line + 1, :], (8, BLOCK))


def eliminate(a, base, one, aside=()):
    groups = len(a)
    a = list(a)
    line = lax.broadcasted_iota(jnp.int32, (8, BLOCK), 0)
    lane = lax.broadcasted_iota(jnp.int32, (8, BLOCK), 1)

    def spread(v, first):
        columns = [over(a[v], first + m) for m in range(8)]
        return [columns[0] * one, columns[1] * one] + columns[2:]

    result = []
    panel, under = spread(0, base), spread(1, base)
    for v0 in range(groups):
        if v0 < len(aside):
            aside[v0]()
        first = base + 8 * v0
        more = v0 + 1 < groups
        inside = (lane >= first) & (lane < first + 8)
        if more:
            ahead = [over(a[v0 + 1], first + 8 + m) for m in range(8)]
            columns = [under] + [[over(a[v], first + m) for m in range(8)] for v in range(v0 + 2, groups)]
            rest = list(under)
        rows = jnp.where(inside, jnp.where(lane == line + first, 1.0, 0.0).astype(jnp.float32), a[v0])
        ratios, pivots = [None] * 8, {}
        for j in range(0, 8, 2):
            p, q, r = down(panel[j], j), down(panel[j], j + 1), down(panel[j + 1], j + 1)
            determinant = p * r - q * q
            inverse = 1.0 / determinant
            pi, qi, ri = p * inverse, q * inverse, r * inverse
            pivots[j] = (p, q, r, pi, qi, ri, determinant)
            if more:
                ratios[j] = rest[j] * ri - rest[j + 1] * qi
                ratios[j + 1] = rest[j + 1] * pi - rest[j] * qi
            if j < 6:
                left = jnp.where(line > j + 1, panel[j] * ri - panel[j + 1] * qi, 0.0)
                right = jnp.where(line > j + 1, panel[j + 1] * pi - panel[j] * qi, 0.0)
                for m in range(j + 2, 8):
                    upper, lower = down(panel[m], j), down(panel[m], j + 1)
                    panel[m] = panel[m] - (left * upper + right * lower)
                    if more:
                        rest[m] = rest[m] - (ratios[j] * upper + ratios[j + 1] * lower)
                rows = rows - (left * down(rows, j) + right * down(rows, j + 1))
        scaled, solved = rows, []
        for j in range(0, 8, 2):
            p, q, r, pi, qi, ri, determinant = pivots[j]
            upper, lower = down(rows, j), down(rows, j + 1)
            root = lax.rsqrt(p)
            square = root * root
            scaled = jnp.where(line == j, upper * root, scaled)
            scaled = jnp.where(
                line == j + 1, (lower - q * square * upper) * lax.rsqrt(determinant * square), scaled
            )
            solved.append((ri * upper - qi * lower, pi * lower - qi * upper))
        result.append(scaled)
        if more:
            following = [
                ahead[m] - add_up([ratios[j] * down(rest[j], m) for j in range(8)]) for m in range(8)
            ]
            change = [None] * 8
            for j in range(6, -1, -2):
                upper, lower = solved[j // 2]
                if j < 6:
                    p, q, r, pi, qi, ri, determinant = pivots[j]
                    first_sum = add_up([down(panel[m], j) * change[m] for m in range(j + 2, 8)])
                    second_sum = add_up([down(panel[m], j + 1) * change[m] for m in range(j + 2, 8)])
                    upper = upper - (ri * first_sum - qi * second_sum)
                    lower = lower - (pi * second_sum - qi * first_sum)
                change[j], change[j + 1] = upper, lower
            for index, v in enumerate(range(v0 + 1, groups)):
                a[v] = jnp.where(inside, 0.0, a[v]) - add_up([columns[index][m] * change[m] for m in range(8)])
            panel = following
            if v0 + 2 < groups:
                under = spread(v0 + 2, first + 8)
    return result


def inverse_factor(matrix, one, aside=()):
    lane = lax.broadcasted_iota(jnp.int32, (8, BLOCK), 1)
    half = BLOCK // 2
    groups = [matrix[8 * v:8 * v + 8, :] for v in range(BLOCK // 8)]
    top = eliminate(groups[:8], 0, one, aside[:8])
    top = [jnp.where((lane < 8 * v + 8) | (lane >= half), rows, 0.0) for v, rows in enumerate(top)]
    beyond = [jnp.where(lane >= half, rows, 0.0) for rows in top]
    change = lax.dot_general(
        jnp.concatenate(beyond, axis=0), jnp.concatenate(top, axis=0), (((0,), (0,)), ((), ())),
        precision=lax.Precision.HIGHEST, preferred_element_type=jnp.float32,
    )
    bottom = [
        jnp.where(lane >= half, rows, 0.0) - change[half + 8 * v:half + 8 * v + 8, :]
        for v, rows in enumerate(groups[8:])
    ]
    bottom = eliminate(bottom, half, one, aside[8:])
    bottom = [jnp.where(lane < half + 8 * v + 8, rows, 0.0) for v, rows in enumerate(bottom)]
    return [jnp.where(lane < half, rows, 0.0) for rows in top] + bottom


def basis_kernel(
    gram_ref, stats_ref, basis_ref, high, low, factor_hbm, core_hbm, turned, image, inverse, factor_ref, core_ref, sems
):
    rows, rank = basis_ref.shape
    blocks = rows // BLOCK
    highest = lax.Precision.HIGHEST
    for b in range(blocks):
        turned[:, b * BLOCK:(b + 1) * BLOCK] = basis_ref[pl.ds(b * BLOCK, BLOCK), :].T
    one = stats_ref[16:24, :]

    def orthonormal(target, aside=()):
        small = dot_nt(image[...], image[...], precision=highest)
        for v, group in enumerate(inverse_factor(small, one, aside)):
            inverse[pl.ds(8 * v, 8), :] = group
        return jnp.dot(inverse[...], target[...], precision=highest, preferred_element_type=jnp.float32)

    def body(iteration, carry):
        def chunk(part):
            window = pl.ds(256 * part, 256)
            turned[:, window] = jnp.dot(
                image[...], gram_ref[:, window], precision=highest, preferred_element_type=jnp.float32
            )

        todo = [functools.partial(chunk, part) for part in range(2)]
        image[...] = orthonormal(turned, [todo[v // 8] if v % 8 == 0 else (lambda: None) for v in range(16)])
        return carry

    image[...] = jnp.dot(turned[...], gram_ref[...], precision=highest, preferred_element_type=jnp.float32)
    lax.fori_loop(0, ITERS - 1, body, 0)
    turned[...] = orthonormal(image)

    constant = None
    for b in range(blocks):
        window = pl.ds(b * BLOCK, BLOCK)
        value = turned[:, window]
        factor_ref[window, :] = value.T
        value = value * stats_ref[4 + b:5 + b, :]
        image[:, window] = value
        term = value * stats_ref[8 + b:9 + b, :]
        constant = term if constant is None else constant + term
    slabs = core_ref.shape[0]
    stores = [pltpu.make_async_copy(factor_ref, factor_hbm, sems.at[slabs])]
    stores[0].start()
    constant = jnp.broadcast_to(jnp.sum(constant, axis=1, keepdims=True), (rank, BLOCK))
    top, rest = split(image[...])
    for s in range(0, slabs, 2):
        window = pl.ds(s * BLOCK, 2 * BLOCK)
        value = jnp.dot(top, high[:, window], preferred_element_type=jnp.float32)
        value = value + jnp.dot(top, low[:, window], preferred_element_type=jnp.float32)
        value = value + jnp.dot(rest, high[:, window], preferred_element_type=jnp.float32)
        core_ref[s] = value[:, :BLOCK] + constant
        core_ref[s + 1] = value[:, BLOCK:] + constant
        for slab in (s, s + 1):
            stores.append(pltpu.make_async_copy(core_ref.at[slab], core_hbm.at[:, slab, :], sems.at[slab]))
            stores[-1].start()
    for store in stores:
        store.wait()


def basis_call(gram_matrix, stats, basis, high, low, slabs):
    rows, rank = basis.shape
    f32 = jnp.float32
    vmem = pl.BlockSpec(memory_space=pltpu.VMEM)
    return pl.pallas_call(
        basis_kernel,
        out_shape=(
            jax.ShapeDtypeStruct((rows, rank), f32),
            jax.ShapeDtypeStruct((rank, slabs, BLOCK), f32),
        ),
        in_specs=[vmem] * 5,
        out_specs=(pl.BlockSpec(memory_space=pl.ANY),) * 2,
        scratch_shapes=[
            pltpu.VMEM((rank, rows), f32),
            pltpu.VMEM((rank, rows), f32),
            pltpu.VMEM((rank, rank), f32),
            pltpu.VMEM((rows, rank), f32),
            pltpu.VMEM((slabs, rank, BLOCK), f32),
            pltpu.SemaphoreType.DMA((slabs + 1,)),
        ],
        compiler_params=pltpu.CompilerParams(vmem_limit_bytes=16 << 20),
    )(gram_matrix, stats, basis, high, low)


def local_step(sizes, tensor, initial_basis):
    cells = float(tensor.shape[1] * tensor.shape[2] * lax.axis_size("row") * lax.axis_size("col"))
    gram_matrix, stats, high, low = gram_call(tensor, sizes, cells)
    return basis_call(gram_matrix, stats, initial_basis, high, low, tensor.shape[1])


def solution(mesh):
    nx = CHIPS_X
    sizes = (nx, mesh.shape["row"] // nx, mesh.shape["col"] // 2)
    in_specs = (P(None, "row", "col"), P())
    out_specs = (P(), P(None, "row", "col"))
    return jax.shard_map(
        functools.partial(local_step, sizes), mesh=mesh, in_specs=in_specs, out_specs=out_specs, check_vma=False
    )
```
